256 devices in a mesh: depth: 32 (over y_lo, z, core), shot: 8 (over x, y_hi).
Axes of the slice: x: 4, y: 4 (y_hi: 2, y_lo: 2; y = y_hi * 2 + y_lo), z: 8, core: 2. Of those that a mesh axis runs over, the one named last changes fastest.
Arguments:
- down_state: bfloat16 [64, 16, 2, 256, 256], P('depth', 'shot'), may hold values from -6 to 6
- up_state: bfloat16 [64, 16, 2, 256, 256], P('depth', 'shot'), may hold values from -6 to 6
- source: bfloat16 [16, 2, 256, 256], P('shot'), may hold values from -6 to 6
- reflect: float32 [64, 256, 256], P('depth'), may hold values from -0.3 to 0.3
- screen_class: int32 [64, 256, 256], P('depth'), may hold values from 0 to 15
- screen_values: float32 [16], replicated, may hold values from -1 to 1
- freq_index: int32 [16], P('shot'), may hold values from 0 to 127
Outputs:
- down_out: bfloat16 [64, 16, 2, 256, 256], P('depth', 'shot')
- up_out: bfloat16 [64, 16, 2, 256, 256], P('depth', 'shot')
- gradient: float32 [64, 256, 256], P('depth', 'shot')
The draws below stay inside these ranges and needn't reach their ends.
All inputs are finite; a program needn't handle non-finite values.
Results may differ from the reference program's by a relative error of at most 0.034.
Values may be sent and summed in bfloat16 or wider, within the bound.
A program may use at most 64 MiB of HBM per device.

```python
import math
import jax
import jax.numpy as jnp
from jax import lax

NX = 256
NY = 256
HOPS = 3
NCLASS = 16
NFREQ = 128
NZ = 64
FRONTS = 16


def with_ends(entries, rng, low, high):
    spot = [jax.random.randint(jax.random.fold_in(rng, axis), (), 0, length) for axis, length in enumerate(entries.shape)]
    main_axis = entries.shape.index(max(entries.shape))
    beside = spot[:main_axis] + [(spot[main_axis] + 1) % entries.shape[main_axis]] + spot[main_axis + 1:]
    return entries.at[tuple(spot)].set(low).at[tuple(beside)].set(high)


def shard_levels(rng, dims, split, least, high):
    def one(position, blocks):
        draws = jax.random.uniform(jax.random.fold_in(jax.random.fold_in(rng, 6), position), (blocks,), jnp.float32, least / len(split), high / len(split))
        return jnp.repeat(jnp.exp(draws), dims[position] // blocks).reshape((-1,) + (1,) * (len(dims) - position - 1))

    loudness = one(*split[0])
    for cut in split[1:]:
        loudness = loudness * one(*cut)
    return loudness


def normal_values(key, dims, spread, reach, split=(), kind=jnp.bfloat16):
    array = spread * jax.random.normal(key, dims, jnp.float32)
    if split:
        array = array * shard_levels(key, dims, split, -0.22, 0.18)
    return jnp.clip(array, -reach, reach).astype(kind)


def setup_inputs(seed: int = 0) -> dict:
    splits = jax.random.split(jax.random.key(seed), 8)
    return {
        "down_state": normal_values(splits[0], (NZ, FRONTS, 2, NX, NY), 1.0, 6.0, ((0, 32), (1, 8))),
        "up_state": normal_values(splits[1], (NZ, FRONTS, 2, NX, NY), 1.0, 6.0, ((0, 32), (1, 8))),
        "source": normal_values(splits[2], (FRONTS, 2, NX, NY), 1.0, 6.0, ((0, 8),)),
        "reflect": jnp.clip(jax.random.uniform(splits[3], (NZ, NX, NY), jnp.float32, -0.3, 0.3) * shard_levels(splits[3], (NZ, NX, NY), ((0, 32),), -0.4, 0.0), -0.3, 0.3),
        "screen_class": with_ends(jax.random.randint(splits[4], (NZ, NX, NY), 0, NCLASS), jax.random.fold_in(splits[4], 1), 0, NCLASS - 1).astype(jnp.int32),
        "screen_values": jnp.clip(jax.random.uniform(splits[5], (NCLASS,), jnp.float32, -1.0, 1.0), -1.0, 1.0),
        "freq_index": with_ends(jax.random.randint(splits[6], (FRONTS,), 0, NFREQ), jax.random.fold_in(splits[6], 1), 0, NFREQ - 1).astype(jnp.int32),
    }


def dft_tables(length):
    counter = jnp.arange(length, dtype=jnp.int32)
    product = counter[:, None] * counter[None, :] % length
    angles = 2.0 * math.pi / length * product.astype(jnp.float32)
    return (jnp.cos(angles).astype(jnp.bfloat16), jnp.sin(angles).astype(jnp.bfloat16))

def wavenumbers(length):
    counter = jnp.arange(length, dtype=jnp.int32)
    wrapped = jnp.where(counter >= length // 2, counter - length, counter)
    return 2.0 * math.pi / length * wrapped.astype(jnp.float32)

def left_mul(matrix, planes):
    return jnp.einsum('jk,...kl->...jl', matrix.astype(jnp.float32), planes.astype(jnp.float32))

def right_mul(planes, matrix):
    return jnp.einsum('...jk,kl->...jl', planes.astype(jnp.float32), matrix.astype(jnp.float32))

def propagate(planes, phase_re, phase_im, cos_x, sin_x, cos_y, sin_y):
    real_in = planes[:, 0]
    imag_in = planes[:, 1]
    first_re = (left_mul(cos_x, real_in) + left_mul(sin_x, imag_in)).astype(jnp.bfloat16)
    first_im = (left_mul(cos_x, imag_in) - left_mul(sin_x, real_in)).astype(jnp.bfloat16)
    second_re = right_mul(first_re, cos_y) + right_mul(first_im, sin_y)
    second_im = right_mul(first_im, cos_y) - right_mul(first_re, sin_y)
    turned_re = (second_re * phase_re - second_im * phase_im).astype(jnp.bfloat16)
    turned_im = (second_re * phase_im + second_im * phase_re).astype(jnp.bfloat16)
    third_re = (left_mul(cos_x, turned_re) - left_mul(sin_x, turned_im)).astype(jnp.bfloat16)
    third_im = (left_mul(sin_x, turned_re) + left_mul(cos_x, turned_im)).astype(jnp.bfloat16)
    final_re = (right_mul(third_re, cos_y) - right_mul(third_im, sin_y)).astype(jnp.bfloat16)
    final_im = (right_mul(third_re, sin_y) + right_mul(third_im, cos_y)).astype(jnp.bfloat16)
    return (final_re.astype(jnp.float32), final_im.astype(jnp.float32))

def reference(down_state, up_state, source, reflect, screen_class, screen_values, freq_index):
    cos_x, sin_x = dft_tables(NX)
    cos_y, sin_y = dft_tables(NY)
    kwave = 0.95 * math.pi * (freq_index.astype(jnp.float32) + 1.0) / NFREQ
    kx_wave = wavenumbers(NX)
    ky_wave = wavenumbers(NY)
    vertical = kwave[:, None, None] ** 2 - kx_wave[None, :, None] ** 2 - ky_wave[None, None, :] ** 2
    propag = jnp.sqrt(jnp.maximum(vertical, 0.0))
    damping = jnp.exp(-jnp.sqrt(jnp.maximum(-vertical, 0.0))) / (NX * NY)
    phase_re = damping * jnp.cos(propag)
    phase_im = damping * jnp.sin(propag)
    slowness = screen_values[screen_class]
    scale = 1.0 / math.sqrt(FRONTS)

    def level(items):
        above, below, refl, slow = items
        angle = kwave[:, None, None] * slow[None]
        screen_re = jnp.cos(angle)
        screen_im = jnp.sin(angle)
        qa_re, qa_im = propagate(above, phase_re, phase_im, cos_x, sin_x, cos_y, sin_y)
        qb_re, qb_im = propagate(below, phase_re, phase_im, cos_x, sin_x, cos_y, sin_y)
        a_re = screen_re * qa_re - screen_im * qa_im
        a_im = screen_re * qa_im + screen_im * qa_re
        b_re = screen_re * qb_re - screen_im * qb_im
        b_im = screen_re * qb_im + screen_im * qb_re
        new_down = jnp.stack([(1.0 + refl) * a_re - refl * b_re, (1.0 + refl) * a_im - refl * b_im], axis=1).astype(jnp.bfloat16)
        new_up = jnp.stack([(1.0 - refl) * b_re + refl * a_re, (1.0 - refl) * b_im + refl * a_im], axis=1).astype(jnp.bfloat16)
        grad = scale * lax.optimization_barrier(jnp.sum(a_re * b_re + a_im * b_im, axis=0))
        return (new_down, new_up, grad)
    down = down_state
    up = up_state
    grad = jnp.zeros((NZ, NX, NY), jnp.float32)
    for repeat in range(HOPS):
        from_above = jnp.concatenate([source[None], down[:-1]], axis=0)
        from_below = jnp.concatenate([up[1:], jnp.zeros_like(up[:1])], axis=0)
        down, up, grad = lax.map(level, (from_above, from_below, reflect, slowness))
    return (down, up, grad)
```

```python
import math

import jax
import jax.numpy as jnp
import numpy as np
from jax import lax
from jax.experimental import pallas as pl
from jax.experimental.pallas import tpu as pltpu
from jax.sharding import PartitionSpec as P

HOPS = 3
NCLASS = 16
NFREQ = 128
N = 256
H = N // 2
MESH = pl.DeviceIdType.MESH
BF16 = jnp.bfloat16
F32 = jnp.float32
COS_COEFS = [(-1.0) ** k / math.factorial(2 * k) for k in range(10)]
SIN_COEFS = [(-1.0) ** k / math.factorial(2 * k + 1) for k in range(10)]


def half_tables():
    row = np.arange(H)[:, None]
    col = np.arange(H)[None, :]
    mats = []
    for parity in (0, 1):
        angle = (2.0 * math.pi / N) * (((2 * row + parity) * col) % N).astype(np.float64)
        cos, sin = np.cos(angle), np.sin(angle)
        fwd = np.block([[cos, sin], [-sin, cos]])
        mats.append(fwd)
        mats.append(fwd.T)
    return np.stack(mats).astype(np.float32)


def poly(coefs, q):
    acc = jnp.full_like(q, coefs[-1])
    for c in coefs[-2::-1]:
        acc = acc * q + c
    return acc


def dot(a, b):
    return jnp.dot(a, b, preferred_element_type=F32)


def kernel(
    groups,
    slabs,
    screen_values,
    freq_index,
    down_hbm,
    up_hbm,
    source_hbm,
    reflect_hbm,
    class_hbm,
    table_hbm,
    down_out,
    up_out,
    grad_out,
    tab,
    classes,
    refl,
    local,
    halo,
    edge,
    inner,
    phase,
    screen,
    lut,
    s2,
    s3,
    s4,
    gsum,
    gsend,
    grecv,
    load_sem,
    src_sem,
    send_sem,
    recv_sem,
    gsend_sem,
    grecv_sem,
):
    d = lax.axis_index("depth")
    s = lax.axis_index("shot")
    has_above = d > 0
    has_below = d < slabs - 1

    loads = [
        pltpu.make_async_copy(table_hbm, tab, load_sem.at[0]),
        pltpu.make_async_copy(class_hbm, classes, load_sem.at[1]),
        pltpu.make_async_copy(reflect_hbm, refl, load_sem.at[2]),
        pltpu.make_async_copy(down_hbm.at[0], local.at[0], load_sem.at[3]),
        pltpu.make_async_copy(up_hbm.at[1], local.at[1], load_sem.at[4]),
    ]
    for c in loads:
        c.start()

    barrier = pltpu.get_barrier_semaphore()

    @pl.when(has_above)
    def _():
        pl.semaphore_signal(barrier, inc=1, device_id={"depth": d - 1}, device_id_type=MESH)

    @pl.when(has_below)
    def _():
        pl.semaphore_signal(barrier, inc=1, device_id={"depth": d + 1}, device_id_type=MESH)

    for o in range(1, groups):
        pl.semaphore_signal(
            barrier, inc=1, device_id={"shot": lax.rem(s + o, groups)}, device_id_type=MESH
        )
    pl.semaphore_wait(
        barrier, groups - 1 + has_above.astype(jnp.int32) + has_below.astype(jnp.int32)
    )

    def to_below(src, h, f):
        return pltpu.make_async_remote_copy(
            src_ref=src,
            dst_ref=halo.at[h, 0, f],
            send_sem=send_sem.at[h, 0, f],
            recv_sem=recv_sem.at[h, 0, f],
            device_id={"depth": lax.rem(d + 1, slabs)},
            device_id_type=MESH,
        )

    def to_above(src, h, f):
        return pltpu.make_async_remote_copy(
            src_ref=src,
            dst_ref=halo.at[h, 1, f],
            send_sem=send_sem.at[h, 1, f],
            recv_sem=recv_sem.at[h, 1, f],
            device_id={"depth": lax.rem(d + slabs - 1, slabs)},
            device_id_type=MESH,
        )

    def from_source(h, f):
        return pltpu.make_async_copy(source_hbm.at[f], halo.at[h, 0, f], src_sem.at[h, f])

    for f in range(2):

        @pl.when(has_below)
        def _():
            to_below(down_hbm.at[1, f], 0, f).start()

        @pl.when(has_above)
        def _():
            to_above(up_hbm.at[0, f], 0, f).start()

    @pl.when(jnp.logical_not(has_above))
    def _():
        for h in range(HOPS):
            for f in range(2):
                from_source(h, f).start()

    @pl.when(jnp.logical_not(has_below))
    def _():
        def clear(t, carry):
            halo[t // 2, 1, lax.rem(t, 2)] = jnp.zeros((2, N, N), BF16)
            return carry

        lax.fori_loop(0, 2 * HOPS, clear, 0)

    kwave = [0.95 * math.pi * (freq_index[f].astype(F32) + 1.0) / NFREQ for f in range(2)]

    def fill_phase(t, carry):
        r0 = pl.multiple_of(t * 8, 8)
        row = lax.broadcasted_iota(jnp.int32, (8, N), 0) + r0
        lane = lax.broadcasted_iota(jnp.int32, (8, N), 1)
        ym = jnp.where(lane < H, 2 * lane, 2 * (lane - H) + 1)
        ym = jnp.where(ym >= H, ym - N, ym)
        ky = (2.0 * math.pi / N) * ym.astype(F32)
        for par in range(2):
            xm = 2 * row + par
            xm = jnp.where(xm >= H, xm - N, xm)
            kx = (2.0 * math.pi / N) * xm.astype(F32)
            k2 = kx * kx + ky * ky
            for f in range(2):
                q = kwave[f] * kwave[f] - k2
                root = jnp.sqrt(jnp.abs(q))
                qp = jnp.maximum(q, 0.0)
                damp = jnp.where(q < 0.0, jnp.exp(-root), 1.0) * (1.0 / (N * N))
                sin = jnp.where(q > 0.0, root, 0.0) * poly(SIN_COEFS, qp)
                phase[f, par, 0, pl.ds(r0, 8), :] = damp * poly(COS_COEFS, qp)
                phase[f, par, 1, pl.ds(r0, 8), :] = damp * sin
        return carry

    lax.fori_loop(0, H // 8, fill_phase, 0)

    for f in range(2):
        for c in range(NCLASS):
            ang = jnp.full((8, 128), kwave[f] * screen_values[c], F32)
            q = ang * ang
            lut[2 * f, c] = poly(COS_COEFS, q)
            lut[2 * f + 1, c] = ang * poly(SIN_COEFS, q)

    loads[1].wait()

    def fill_screen(t, carry):
        lev = t // (N // 8)
        r0 = pl.multiple_of(lax.rem(t, N // 8) * 8, 8)
        for half in range(2):
            cols = pl.ds(half * H, H)
            cls = classes[lev, pl.ds(r0, 8), cols]
            bits = [(cls & (1 << b)) != 0 for b in range(4)]
            for k in range(4):
                vals = [lut[k, c] for c in range(NCLASS)]
                for b in range(4):
                    vals = [
                        jnp.where(bits[b], vals[2 * i + 1], vals[2 * i])
                        for i in range(len(vals) // 2)
                    ]
                screen[lev, k // 2, k % 2, pl.ds(r0, 8), cols] = vals[0]
        return carry

    lax.fori_loop(0, 2 * N // 8, fill_screen, 0)
    loads[0].wait()
    loads[2].wait()
    loads[3].wait()
    loads[4].wait()

    def propagate(srcs, f):
        fe, ie, fo, io = 0, 1, 2, 3
        for i, src in enumerate(srcs):
            re_l, re_r = src[0, :, :H], src[0, :, H:]
            im_l, im_r = src[1, :, :H], src[1, :, H:]
            ev = dot(jnp.concatenate([re_l + re_r, im_l + im_r], axis=1), tab[ie])
            od = dot(jnp.concatenate([re_l - re_r, im_l - im_r], axis=1), tab[io])
            for j, x in enumerate((ev, od)):
                cols = slice(j * H, (j + 1) * H)
                u = (x[:H] + x[H:]).astype(BF16)
                v = (x[:H] - x[H:]).astype(BF16)
                s2[i, 0, :H, cols] = u[:, :H]
                s2[i, 0, H:, cols] = u[:, H:]
                s2[i, 1, :H, cols] = v[:, :H]
                s2[i, 1, H:, cols] = v[:, H:]
        for i in range(len(srcs)):
            for par, t in enumerate((fe, fo)):
                x = dot(tab[t], s2[i, par])
                pr, pi = phase[f, par, 0], phase[f, par, 1]
                re, im = x[:H], x[H:]
                s3[i, par, :H] = (re * pr - im * pi).astype(BF16)
                s3[i, par, H:] = (re * pi + im * pr).astype(BF16)
        for i in range(len(srcs)):
            e = dot(tab[ie], s3[i, 0])
            o = dot(tab[io], s3[i, 1])
            top = (e + o).astype(BF16)
            bot = (e - o).astype(BF16)
            for j in range(2):
                cols = slice(j * H, (j + 1) * H)
                s4[i, j, :H, :H] = top[:H, cols]
                s4[i, j, :H, H:] = top[H:, cols]
                s4[i, j, H:, :H] = bot[:H, cols]
                s4[i, j, H:, H:] = bot[H:, cols]
        outs = []
        for i in range(len(srcs)):
            e = dot(s4[i, 0], tab[fe])
            o = dot(s4[i, 1], tab[fo])
            outs.append((e + o, e - o))
        return outs

    def screened(x, lev, f, j):
        cols = slice(j * H, (j + 1) * H)
        sr, si = screen[lev, f, 0, :, cols], screen[lev, f, 1, :, cols]
        re, im = x[j][:, :H], x[j][:, H:]
        return (sr * re - si * im, sr * im + si * re)

    def inner_step(f):
        qa, qb = propagate((local.at[0, f], local.at[1, f]), f)
        for j in range(2):
            cols = slice(j * H, (j + 1) * H)
            for k, (x, lev) in enumerate(((qa, 1), (qb, 0))):
                re, im = screened(x, lev, f, j)
                inner[k, f, 0, :, cols] = re
                inner[k, f, 1, :, cols] = im

    def wait_halo(h, f):
        @pl.when(has_above)
        def _():
            to_below(halo.at[h, 0, f], h, f).wait_recv()

        @pl.when(jnp.logical_not(has_above))
        def _():
            from_source(h, f).wait()

        @pl.when(has_below)
        def _():
            to_above(halo.at[h, 1, f], h, f).wait_recv()

    def outer_step(h, f, dn1, up1, dn0, up0, grad):
        wait_halo(h, f)
        qa, qb = propagate((halo.at[h, 0, f], halo.at[h, 1, f]), f)
        for j in range(2):
            cols = slice(j * H, (j + 1) * H)
            a0 = screened(qa, 0, f, j)
            b1 = screened(qb, 1, f, j)
            r0, r1 = refl[0, :, cols], refl[1, :, cols]
            g0 = g1 = 0.0
            for c in range(2):
                b0 = inner[1, f, c, :, cols]
                a1 = inner[0, f, c, :, cols]
                t0 = r0 * (a0[c] - b0)
                t1 = r1 * (a1 - b1[c])
                dn1[c, :, cols] = (a1 + t1).astype(BF16)
                up0[c, :, cols] = (b0 + t0).astype(BF16)
                dn0[c, :, cols] = (a0[c] + t0).astype(BF16)
                up1[c, :, cols] = (b1[c] + t1).astype(BF16)
                g0 = g0 + a0[c] * b0
                g1 = g1 + a1 * b1[c]
            if grad is not None:
                grad(j, g0, g1)

    def first(f, carry):
        inner_step(f)
        return carry

    lax.fori_loop(0, 2, first, 0)

    def middle(t, carry):
        h, f = t // 2, lax.rem(t, 2)
        outer_step(
            h, f, edge.at[h, 0, f], local.at[1, f], local.at[0, f], edge.at[h, 1, f], None
        )

        @pl.when(has_below)
        def _():
            to_below(edge.at[h, 0, f], h + 1, f).start()

        @pl.when(has_above)
        def _():
            to_above(edge.at[h, 1, f], h + 1, f).start()

        inner_step(f)
        return carry

    lax.fori_loop(0, 2 * (HOPS - 1), middle, 0)

    scale = 1.0 / math.sqrt(2 * groups)

    def grad_first(j, g0, g1):
        cols = slice(j * H, (j + 1) * H)
        gsum[0, :, cols] = g0
        gsum[1, :, cols] = g1

    def grad_last(j, g0, g1):
        cols = slice(j * H, (j + 1) * H)
        rows = N // groups
        for lev, g in enumerate((g0, g1)):
            tot = ((gsum[lev, :, cols] + g) * scale).astype(BF16)
            for k in range(groups):
                gsend[k, lev, :, cols] = tot[k * rows : (k + 1) * rows]

    for f in range(2):
        outer_step(
            HOPS - 1,
            f,
            down_out.at[1, f],
            up_out.at[1, f],
            down_out.at[0, f],
            up_out.at[0, f],
            grad_last if f else grad_first,
        )

    def share(o):
        peer = lax.rem(s + o, groups)
        return pltpu.make_async_remote_copy(
            src_ref=gsend.at[peer],
            dst_ref=grecv.at[o - 1],
            send_sem=gsend_sem.at[o - 1],
            recv_sem=grecv_sem.at[o - 1],
            device_id={"shot": peer},
            device_id_type=MESH,
        )

    for o in range(1, groups):
        share(o).start()

    for h in range(HOPS):
        for f in range(2):

            @pl.when(has_below)
            def _():
                to_below(edge.at[0, 0, f], h, f).wait_send()

            @pl.when(has_above)
            def _():
                to_above(edge.at[0, 1, f], h, f).wait_send()

    total = gsend[s].astype(F32)
    for o in range(1, groups):
        share(o).wait_recv()
        total = total + grecv[o - 1].astype(F32)
    grad_out[...] = total
    for o in range(1, groups):
        share(o).wait_send()


def solution(mesh):
    groups = mesh.shape["shot"]
    slabs = mesh.shape["depth"]
    rows = N // groups

    def per_device(down_state, up_state, source, reflect, screen_class, screen_values, freq_index):
        table = jnp.asarray(half_tables(), BF16)
        hbm = pl.BlockSpec(memory_space=pl.ANY)
        smem = pl.BlockSpec(memory_space=pltpu.SMEM)
        vmem = pl.BlockSpec(memory_space=pltpu.VMEM)
        dma = pltpu.SemaphoreType.DMA
        return pl.pallas_call(
            lambda *refs: kernel(groups, slabs, *refs),
            out_shape=(
                jax.ShapeDtypeStruct(down_state.shape, BF16),
                jax.ShapeDtypeStruct(up_state.shape, BF16),
                jax.ShapeDtypeStruct((2, rows, N), F32),
            ),
            in_specs=[smem, smem, hbm, hbm, hbm, hbm, hbm, hbm],
            out_specs=(vmem, vmem, vmem),
            scratch_shapes=[
                pltpu.VMEM((4, N, N), BF16),
                pltpu.VMEM((2, N, N), jnp.int32),
                pltpu.VMEM((2, N, N), F32),
                pltpu.VMEM((2, 2, 2, N, N), BF16),
                pltpu.VMEM((HOPS, 2, 2, 2, N, N), BF16),
                pltpu.VMEM((HOPS - 1, 2, 2, 2, N, N), BF16),
                pltpu.VMEM((2, 2, 2, N, N), F32),
                pltpu.VMEM((2, 2, 2, H, N), F32),
                pltpu.VMEM((2, 2, 2, N, N), F32),
                pltpu.VMEM((4, NCLASS, 8, 128), F32),
                pltpu.VMEM((2, 2, N, N), BF16),
                pltpu.VMEM((2, 2, N, N), BF16),
                pltpu.VMEM((2, 2, N, N), BF16),
                pltpu.VMEM((2, N, N), F32),
                pltpu.VMEM((groups, 2, rows, N), BF16),
                pltpu.VMEM((groups - 1, 2, rows, N), BF16),
                dma((5,)),
                dma((HOPS, 2)),
                dma((HOPS, 2, 2)),
                dma((HOPS, 2, 2)),
                dma((groups - 1,)),
                dma((groups - 1,)),
            ],
            compiler_params=pltpu.CompilerParams(
                collective_id=0, has_side_effects=True, vmem_limit_bytes=56 * 1024 * 1024
            ),
        )(screen_values, freq_index, down_state, up_state, source, reflect, screen_class, table)

    return jax.shard_map(
        per_device,
        mesh=mesh,
        in_specs=(
            P("depth", "shot", None, None, None),
            P("depth", "shot", None, None, None),
            P("shot", None, None, None),
            P("depth", None, None),
            P("depth", None, None),
            P(),
            P("shot"),
        ),
        out_specs=(
            P("depth", "shot", None, None, None),
            P("depth", "shot", None, None, None),
            P("depth", "shot", None),
        ),
        check_vma=False,
    )
```

```python
import math

import jax
import jax.numpy as jnp
import numpy as np
from jax import lax
from jax.experimental import pallas as pl
from jax.experimental.pallas import tpu as pltpu
from jax.sharding import PartitionSpec as P

HOPS = 3
NCLASS = 16
NFREQ = 128
N = 256
H = N // 2
MESH = pl.DeviceIdType.MESH
BF16 = jnp.bfloat16
F32 = jnp.float32
COS_COEFS = [(-1.0) ** k / math.factorial(2 * k) for k in range(10)]
SIN_COEFS = [(-1.0) ** k / math.factorial(2 * k + 1) for k in range(10)]


def half_tables():
    row = np.arange(H)[:, None]
    col = np.arange(H)[None, :]
    mats = []
    for parity in (0, 1):
        angle = (2.0 * math.pi / N) * (((2 * row + parity) * col) % N).astype(np.float64)
        cos, sin = np.cos(angle), np.sin(angle)
        fwd = np.block([[cos, sin], [-sin, cos]])
        mats.append(fwd)
        mats.append(fwd.T)
    return np.stack(mats).astype(np.float32)


def poly(coefs, q):
    acc = jnp.full_like(q, coefs[-1])
    for c in coefs[-2::-1]:
        acc = acc * q + c
    return acc


def dot(a, b):
    return jnp.dot(a, b, preferred_element_type=F32)


def kernel(
    groups,
    slabs,
    values_hbm,
    freq_hbm,
    down_hbm,
    up_hbm,
    source_hbm,
    reflect_hbm,
    class_hbm,
    table_hbm,
    down_out,
    up_out,
    grad_out,
    tab,
    classes,
    refl,
    local,
    halo,
    edge,
    inner,
    phase,
    screen,
    lut,
    s2,
    s3,
    s4,
    gsum,
    gsend,
    grecv,
    screen_values,
    freq_index,
    load_sem,
    src_sem,
    send_sem,
    recv_sem,
    gsend_sem,
    grecv_sem,
    near_sem,
):
    d = lax.axis_index("depth")
    s = lax.axis_index("shot")
    has_above = d > 0
    has_below = d < slabs - 1

    loads = [
        pltpu.make_async_copy(table_hbm, tab, load_sem.at[0]),
        pltpu.make_async_copy(class_hbm, classes, load_sem.at[1]),
        pltpu.make_async_copy(reflect_hbm, refl, load_sem.at[2]),
        pltpu.make_async_copy(down_hbm.at[0], local.at[0], load_sem.at[3]),
        pltpu.make_async_copy(up_hbm.at[1], local.at[1], load_sem.at[4]),
        pltpu.make_async_copy(freq_hbm, freq_index, load_sem.at[5]),
        pltpu.make_async_copy(values_hbm, screen_values, load_sem.at[6]),
    ]
    near = [
        lax.rem(s + 2, groups),
        lax.rem(s + groups - 2, groups),
        s + 1 - 2 * lax.rem(s, 2),
    ]

    def greet(sem):
        for peer in near:
            pl.semaphore_signal(sem, inc=1, device_id={"shot": peer}, device_id_type=MESH)

    barrier = pltpu.get_barrier_semaphore()

    @pl.when(has_above)
    def _():
        pl.semaphore_signal(barrier, inc=1, device_id={"depth": d - 1}, device_id_type=MESH)

    @pl.when(has_below)
    def _():
        pl.semaphore_signal(barrier, inc=1, device_id={"depth": d + 1}, device_id_type=MESH)

    greet(barrier)
    for c in loads[::-1]:
        c.start()
    pl.semaphore_wait(
        barrier, len(near) + has_above.astype(jnp.int32) + has_below.astype(jnp.int32)
    )

    def to_below(src, h, f):
        return pltpu.make_async_remote_copy(
            src_ref=src,
            dst_ref=halo.at[h, 0, f],
            send_sem=send_sem.at[h, 0, f],
            recv_sem=recv_sem.at[h, 0, f],
            device_id={"depth": lax.rem(d + 1, slabs)},
            device_id_type=MESH,
        )

    def to_above(src, h, f):
        return pltpu.make_async_remote_copy(
            src_ref=src,
            dst_ref=halo.at[h, 1, f],
            send_sem=send_sem.at[h, 1, f],
            recv_sem=recv_sem.at[h, 1, f],
            device_id={"depth": lax.rem(d + slabs - 1, slabs)},
            device_id_type=MESH,
        )

    def from_source(h, f):
        return pltpu.make_async_copy(source_hbm.at[f], halo.at[h, 0, f], src_sem.at[h, f])

    for f in range(2):

        @pl.when(has_below)
        def _():
            to_below(down_hbm.at[1, f], 0, f).start()

        @pl.when(has_above)
        def _():
            to_above(up_hbm.at[0, f], 0, f).start()

    @pl.when(jnp.logical_not(has_above))
    def _():
        for h in range(HOPS):
            for f in range(2):
                from_source(h, f).start()

    @pl.when(jnp.logical_not(has_below))
    def _():
        def clear(t, carry):
            halo[t // 2, 1, lax.rem(t, 2)] = jnp.zeros((2, N, N), BF16)
            return carry

        lax.fori_loop(0, 2 * HOPS, clear, 0)

    greet(near_sem.at[0])
    loads[5].wait()
    kwave = [0.95 * math.pi * (freq_index[f].astype(F32) + 1.0) / NFREQ for f in range(2)]

    def fill_phase(t, carry):
        r0 = pl.multiple_of(t * 8, 8)
        row = lax.broadcasted_iota(jnp.int32, (8, N), 0) + r0
        lane = lax.broadcasted_iota(jnp.int32, (8, N), 1)
        ym = jnp.where(lane < H, 2 * lane, 2 * (lane - H) + 1)
        ym = jnp.where(ym >= H, ym - N, ym)
        ky = (2.0 * math.pi / N) * ym.astype(F32)
        for par in range(2):
            xm = 2 * row + par
            xm = jnp.where(xm >= H, xm - N, xm)
            kx = (2.0 * math.pi / N) * xm.astype(F32)
            k2 = kx * kx + ky * ky
            for f in range(2):
                q = kwave[f] * kwave[f] - k2
                root = jnp.sqrt(jnp.abs(q))
                qp = jnp.maximum(q, 0.0)
                damp = jnp.where(q < 0.0, jnp.exp(-root), 1.0) * (1.0 / (N * N))
                sin = jnp.where(q > 0.0, root, 0.0) * poly(SIN_COEFS, qp)
                phase[f, par, 0, pl.ds(r0, 8), :] = damp * poly(COS_COEFS, qp)
                phase[f, par, 1, pl.ds(r0, 8), :] = damp * sin
        return carry

    lax.fori_loop(0, H // 8, fill_phase, 0)

    loads[6].wait()
    for f in range(2):
        for c in range(NCLASS):
            ang = jnp.full((8, 128), kwave[f] * screen_values[c], F32)
            q = ang * ang
            lut[2 * f, c] = poly(COS_COEFS, q)
            lut[2 * f + 1, c] = ang * poly(SIN_COEFS, q)

    loads[1].wait()

    def fill_screen(t, carry):
        lev = t // (N // 8)
        r0 = pl.multiple_of(lax.rem(t, N // 8) * 8, 8)
        for half in range(2):
            cols = pl.ds(half * H, H)
            cls = classes[lev, pl.ds(r0, 8), cols]
            bits = [(cls & (1 << b)) != 0 for b in range(4)]
            for k in range(4):
                vals = [lut[k, c] for c in range(NCLASS)]
                for b in range(4):
                    vals = [
                        jnp.where(bits[b], vals[2 * i + 1], vals[2 * i])
                        for i in range(len(vals) // 2)
                    ]
                screen[lev, k // 2, k % 2, pl.ds(r0, 8), cols] = vals[0]
        return carry

    lax.fori_loop(0, 2 * N // 8, fill_screen, 0)
    loads[0].wait()
    loads[2].wait()
    loads[3].wait()
    loads[4].wait()

    def propagate(srcs, f):
        fe, ie, fo, io = 0, 1, 2, 3
        for i, src in enumerate(srcs):
            re_l, re_r = src[0, :, :H], src[0, :, H:]
            im_l, im_r = src[1, :, :H], src[1, :, H:]
            ev = dot(jnp.concatenate([re_l + re_r, im_l + im_r], axis=1), tab[ie])
            od = dot(jnp.concatenate([re_l - re_r, im_l - im_r], axis=1), tab[io])
            for j, x in enumerate((ev, od)):
                cols = slice(j * H, (j + 1) * H)
                u = (x[:H] + x[H:]).astype(BF16)
                v = (x[:H] - x[H:]).astype(BF16)
                s2[i, 0, :H, cols] = u[:, :H]
                s2[i, 0, H:, cols] = u[:, H:]
                s2[i, 1, :H, cols] = v[:, :H]
                s2[i, 1, H:, cols] = v[:, H:]
        for i in range(len(srcs)):
            for par, t in enumerate((fe, fo)):
                x = dot(tab[t], s2[i, par])
                pr, pi = phase[f, par, 0], phase[f, par, 1]
                re, im = x[:H], x[H:]
                s3[i, par, :H] = (re * pr - im * pi).astype(BF16)
                s3[i, par, H:] = (re * pi + im * pr).astype(BF16)
        for i in range(len(srcs)):
            e = dot(tab[ie], s3[i, 0])
            o = dot(tab[io], s3[i, 1])
            top = (e + o).astype(BF16)
            bot = (e - o).astype(BF16)
            for j in range(2):
                cols = slice(j * H, (j + 1) * H)
                s4[i, j, :H, :H] = top[:H, cols]
                s4[i, j, :H, H:] = top[H:, cols]
                s4[i, j, H:, :H] = bot[:H, cols]
                s4[i, j, H:, H:] = bot[H:, cols]
        outs = []
        for i in range(len(srcs)):
            e = dot(s4[i, 0], tab[fe])
            o = dot(s4[i, 1], tab[fo])
            outs.append((e + o, e - o))
        return outs

    def screened(x, lev, f, j):
        cols = slice(j * H, (j + 1) * H)
        sr, si = screen[lev, f, 0, :, cols], screen[lev, f, 1, :, cols]
        re, im = x[j][:, :H], x[j][:, H:]
        return (sr * re - si * im, sr * im + si * re)

    def inner_step(f):
        qa, qb = propagate((local.at[0, f], local.at[1, f]), f)
        for j in range(2):
            cols = slice(j * H, (j + 1) * H)
            for k, (x, lev) in enumerate(((qa, 1), (qb, 0))):
                re, im = screened(x, lev, f, j)
                inner[k, f, 0, :, cols] = re
                inner[k, f, 1, :, cols] = im

    def wait_halo(h, f):
        @pl.when(has_above)
        def _():
            to_below(halo.at[h, 0, f], h, f).wait_recv()

        @pl.when(jnp.logical_not(has_above))
        def _():
            from_source(h, f).wait()

        @pl.when(has_below)
        def _():
            to_above(halo.at[h, 1, f], h, f).wait_recv()

    def outer_step(h, f, dn1, up1, dn0, up0, grad):
        wait_halo(h, f)
        qa, qb = propagate((halo.at[h, 0, f], halo.at[h, 1, f]), f)
        for j in range(2):
            cols = slice(j * H, (j + 1) * H)
            a0 = screened(qa, 0, f, j)
            b1 = screened(qb, 1, f, j)
            r0, r1 = refl[0, :, cols], refl[1, :, cols]
            g0 = g1 = 0.0
            for c in range(2):
                b0 = inner[1, f, c, :, cols]
                a1 = inner[0, f, c, :, cols]
                t0 = r0 * (a0[c] - b0)
                t1 = r1 * (a1 - b1[c])
                dn1[c, :, cols] = (a1 + t1).astype(BF16)
                up0[c, :, cols] = (b0 + t0).astype(BF16)
                dn0[c, :, cols] = (a0[c] + t0).astype(BF16)
                up1[c, :, cols] = (b1[c] + t1).astype(BF16)
                g0 = g0 + a0[c] * b0
                g1 = g1 + a1 * b1[c]
            if grad is not None:
                grad(j, g0, g1)

    def first(f, carry):
        inner_step(f)
        return carry

    lax.fori_loop(0, 2, first, 0)
    pl.semaphore_wait(near_sem.at[0], len(near))
    greet(near_sem.at[1])

    def middle(t, carry):
        h, f = t // 2, lax.rem(t, 2)
        outer_step(
            h, f, edge.at[h, 0, f], local.at[1, f], local.at[0, f], edge.at[h, 1, f], None
        )

        @pl.when(has_below)
        def _():
            to_below(edge.at[h, 0, f], h + 1, f).start()

        @pl.when(has_above)
        def _():
            to_above(edge.at[h, 1, f], h + 1, f).start()

        inner_step(f)
        return carry

    lax.fori_loop(0, 2 * (HOPS - 1), middle, 0)

    scale = 1.0 / math.sqrt(2 * groups)

    def grad_first(j, g0, g1):
        cols = slice(j * H, (j + 1) * H)
        gsum[0, :, cols] = g0
        gsum[1, :, cols] = g1

    def grad_last(j, g0, g1):
        cols = slice(j * H, (j + 1) * H)
        rows = N // groups
        for lev, g in enumerate((g0, g1)):
            tot = ((gsum[lev, :, cols] + g) * scale).astype(BF16)
            for k in range(groups):
                gsend[k, lev, :, cols] = tot[k * rows : (k + 1) * rows]

    for f in range(2):
        outer_step(
            HOPS - 1,
            f,
            down_out.at[1, f],
            up_out.at[1, f],
            down_out.at[0, f],
            up_out.at[0, f],
            grad_last if f else grad_first,
        )

    def share(o):
        peer = lax.rem(s + o, groups)
        return pltpu.make_async_remote_copy(
            src_ref=gsend.at[peer],
            dst_ref=grecv.at[o - 1],
            send_sem=gsend_sem.at[o - 1],
            recv_sem=grecv_sem.at[o - 1],
            device_id={"shot": peer},
            device_id_type=MESH,
        )

    pl.semaphore_wait(near_sem.at[1], len(near))
    for o in range(1, groups):
        share(o).start()

    for h in range(HOPS):
        for f in range(2):

            @pl.when(has_below)
            def _():
                to_below(edge.at[0, 0, f], h, f).wait_send()

            @pl.when(has_above)
            def _():
                to_above(edge.at[0, 1, f], h, f).wait_send()

    total = gsend[s].astype(F32)
    for o in range(1, groups):
        share(o).wait_recv()
        total = total + grecv[o - 1].astype(F32)
    grad_out[...] = total
    for o in range(1, groups):
        share(o).wait_send()


def store(*refs):
    sems = refs[-1]
    copies = [pltpu.make_async_copy(refs[i], refs[i + 3], sems.at[i]) for i in range(3)]
    for c in copies:
        c.start()
    for c in copies:
        c.wait()


def solution(mesh):
    groups = mesh.shape["shot"]
    slabs = mesh.shape["depth"]
    rows = N // groups

    def per_device(down_state, up_state, source, reflect, screen_class, screen_values, freq_index):
        table = jnp.asarray(half_tables(), BF16)
        hbm = pl.BlockSpec(memory_space=pltpu.HBM)
        vmem = pl.BlockSpec(memory_space=pltpu.VMEM)
        dma = pltpu.SemaphoreType.DMA
        results = pl.pallas_call(
            lambda *refs: kernel(groups, slabs, *refs),
            out_shape=(
                pltpu.VMEM(down_state.shape, BF16),
                pltpu.VMEM(up_state.shape, BF16),
                pltpu.VMEM((2, rows, N), F32),
            ),
            in_specs=[hbm] * 8,
            out_specs=(vmem, vmem, vmem),
            scratch_shapes=[
                pltpu.VMEM((4, N, N), BF16),
                pltpu.VMEM((2, N, N), jnp.int32),
                pltpu.VMEM((2, N, N), F32),
                pltpu.VMEM((2, 2, 2, N, N), BF16),
                pltpu.VMEM((HOPS, 2, 2, 2, N, N), BF16),
                pltpu.VMEM((HOPS - 1, 2, 2, 2, N, N), BF16),
                pltpu.VMEM((2, 2, 2, N, N), F32),
                pltpu.VMEM((2, 2, 2, H, N), F32),
                pltpu.VMEM((2, 2, 2, N, N), F32),
                pltpu.VMEM((4, NCLASS, 8, 128), F32),
                pltpu.VMEM((2, 2, N, N), BF16),
                pltpu.VMEM((2, 2, N, N), BF16),
                pltpu.VMEM((2, 2, N, N), BF16),
                pltpu.VMEM((2, N, N), F32),
                pltpu.VMEM((groups, 2, rows, N), BF16),
                pltpu.VMEM((groups - 1, 2, rows, N), BF16),
                pltpu.SMEM((NCLASS,), F32),
                pltpu.SMEM((2,), jnp.int32),
                dma((7,)),
                dma((HOPS, 2)),
                dma((HOPS, 2, 2)),
                dma((HOPS, 2, 2)),
                dma((groups - 1,)),
                dma((groups - 1,)),
                pltpu.SemaphoreType.REGULAR((2,)),
            ],
            compiler_params=pltpu.CompilerParams(
                collective_id=0, has_side_effects=True, vmem_limit_bytes=40 * 1024 * 1024
            ),
        )(
            *(
                pltpu.with_memory_space_constraint(x, pltpu.HBM)
                for x in (
                    screen_values,
                    freq_index,
                    down_state,
                    up_state,
                    source,
                    reflect,
                    screen_class,
                    table,
                )
            ),
        )
        return pl.pallas_call(
            store,
            out_shape=[pltpu.HBM(x.shape, x.dtype) for x in results],
            in_specs=[vmem] * 3,
            out_specs=[hbm] * 3,
            scratch_shapes=[dma((3,))],
        )(*(pltpu.with_memory_space_constraint(x, pltpu.VMEM) for x in results))

    return jax.shard_map(
        per_device,
        mesh=mesh,
        in_specs=(
            P("depth", "shot", None, None, None),
            P("depth", "shot", None, None, None),
            P("shot", None, None, None),
            P("depth", None, None),
            P("depth", None, None),
            P(),
            P("shot"),
        ),
        out_specs=(
            P("depth", "shot", None, None, None),
            P("depth", "shot", None, None, None),
            P("depth", "shot", None),
        ),
        check_vma=False,
    )
```

```python
import math

import jax
import jax.numpy as jnp
import numpy as np
from jax import lax
from jax.experimental import pallas as pl
from jax.experimental.pallas import tpu as pltpu
from jax.sharding import PartitionSpec as P

HOPS = 3
NCLASS = 16
NFREQ = 128
N = 256
H = N // 2
MESH = pl.DeviceIdType.MESH
BF16 = jnp.bfloat16
F32 = jnp.float32
COS_COEFS = [(-1.0) ** k / math.factorial(2 * k) for k in range(10)]
SIN_COEFS = [(-1.0) ** k / math.factorial(2 * k + 1) for k in range(10)]


def half_tables():
    row = np.arange(H)[:, None]
    col = np.arange(H)[None, :]
    mats = []
    for parity in (0, 1):
        angle = (2.0 * math.pi / N) * (((2 * row + parity) * col) % N).astype(np.float64)
        cos, sin = np.cos(angle), np.sin(angle)
        fwd = np.block([[cos, sin], [-sin, cos]])
        mats.append(fwd)
        mats.append(fwd.T)
    return np.stack(mats).astype(np.float32)


def poly(coefs, q):
    acc = jnp.full_like(q, coefs[-1])
    for c in coefs[-2::-1]:
        acc = acc * q + c
    return acc


def dot(a, b):
    return jnp.dot(a, b, preferred_element_type=F32)


def kernel(
    groups,
    slabs,
    values_hbm,
    freq_hbm,
    down_hbm,
    up_hbm,
    source_hbm,
    reflect_hbm,
    class_hbm,
    table_hbm,
    local,
    edge,
    grad_out,
    tab,
    classes,
    refl,
    halo,
    inner,
    phase,
    screen,
    lut,
    s2,
    s3,
    s4,
    gsum,
    gsend,
    grecv,
    screen_values,
    freq_index,
    load_sem,
    src_sem,
    send_sem,
    recv_sem,
    gsend_sem,
    grecv_sem,
    near_sem,
):
    d = lax.axis_index("depth")
    s = lax.axis_index("shot")
    has_above = d > 0
    has_below = d < slabs - 1

    loads = [
        pltpu.make_async_copy(table_hbm, tab, load_sem.at[0]),
        pltpu.make_async_copy(class_hbm, classes, load_sem.at[1]),
        pltpu.make_async_copy(reflect_hbm, refl, load_sem.at[2]),
        pltpu.make_async_copy(down_hbm.at[0], local.at[0], load_sem.at[3]),
        pltpu.make_async_copy(up_hbm.at[1], local.at[1], load_sem.at[4]),
        pltpu.make_async_copy(freq_hbm, freq_index, load_sem.at[5]),
        pltpu.make_async_copy(values_hbm, screen_values, load_sem.at[6]),
    ]
    near = [
        lax.rem(s + 2, groups),
        lax.rem(s + groups - 2, groups),
        s + 1 - 2 * lax.rem(s, 2),
    ]

    def greet(sem):
        for peer in near:
            pl.semaphore_signal(sem, inc=1, device_id={"shot": peer}, device_id_type=MESH)

    barrier = pltpu.get_barrier_semaphore()

    @pl.when(has_above)
    def _():
        pl.semaphore_signal(barrier, inc=1, device_id={"depth": d - 1}, device_id_type=MESH)

    @pl.when(has_below)
    def _():
        pl.semaphore_signal(barrier, inc=1, device_id={"depth": d + 1}, device_id_type=MESH)

    greet(barrier)
    for c in loads[::-1]:
        c.start()

    def link(src, h, k, f):
        return pltpu.make_async_remote_copy(
            src_ref=src,
            dst_ref=halo.at[h, 1 - k, f],
            send_sem=send_sem.at[h, k, f],
            recv_sem=recv_sem.at[h, 1 - k, f],
            device_id={"depth": lax.rem(d + 2 * k + slabs - 1, slabs)},
            device_id_type=MESH,
        )

    def linked(k):
        peer = d + 2 * k - 1
        return jnp.logical_and(peer >= 0, peer < slabs)

    def from_source(h, f):
        return pltpu.make_async_copy(source_hbm.at[f], halo.at[h, 0, f], src_sem.at[h, f])

    late = lax.rem(d, 2)
    early = 1 - late

    def fill_phase(f):
        k0 = 0.95 * math.pi * (freq_index[f].astype(F32) + 1.0) / NFREQ

        def rows(t, carry):
            r0 = pl.multiple_of(t * 8, 8)
            row = lax.broadcasted_iota(jnp.int32, (8, N), 0) + r0
            lane = lax.broadcasted_iota(jnp.int32, (8, N), 1)
            ym = jnp.where(lane < H, 2 * lane, 2 * (lane - H) + 1)
            ym = jnp.where(ym >= H, ym - N, ym)
            ky = (2.0 * math.pi / N) * ym.astype(F32)
            for par in range(2):
                xm = 2 * row + par
                xm = jnp.where(xm >= H, xm - N, xm)
                kx = (2.0 * math.pi / N) * xm.astype(F32)
                q = k0 * k0 - (kx * kx + ky * ky)
                root = jnp.sqrt(jnp.abs(q))
                qp = jnp.maximum(q, 0.0)
                damp = jnp.where(q < 0.0, jnp.exp(-root), 1.0) * (1.0 / (N * N))
                sin = jnp.where(q > 0.0, root, 0.0) * poly(SIN_COEFS, qp)
                phase[f, par, 0, pl.ds(r0, 8), :] = damp * poly(COS_COEFS, qp)
                phase[f, par, 1, pl.ds(r0, 8), :] = damp * sin
            return carry

        lax.fori_loop(0, H // 8, rows, 0)

    def fill_screen(f):
        k0 = 0.95 * math.pi * (freq_index[f].astype(F32) + 1.0) / NFREQ
        for c in range(NCLASS):
            ang = jnp.full((8, 128), k0 * screen_values[c], F32)
            q = ang * ang
            lut[0, c] = poly(COS_COEFS, q)
            lut[1, c] = ang * poly(SIN_COEFS, q)

        def rows(t, carry):
            lev = t // (N // 8)
            r0 = pl.multiple_of(lax.rem(t, N // 8) * 8, 8)
            cls = [classes[lev, pl.ds(r0, 8), pl.ds(j * H, H)] for j in range(2)]
            bits = [[(c & (1 << b)) != 0 for b in range(4)] for c in cls]
            for k in range(2):
                table = [lut[k, c] for c in range(NCLASS)]
                for j in range(2):
                    vals = table
                    for b in range(4):
                        vals = [
                            jnp.where(bits[j][b], vals[2 * i + 1], vals[2 * i])
                            for i in range(len(vals) // 2)
                        ]
                    screen[lev, f, k, pl.ds(r0, 8), pl.ds(j * H, H)] = vals[0]
            return carry

        lax.fori_loop(0, 2 * N // 8, rows, 0)

    loads[5].wait()
    fill_phase(0)
    pl.semaphore_wait(
        barrier, len(near) + has_above.astype(jnp.int32) + has_below.astype(jnp.int32)
    )

    for f in range(2):

        @pl.when(has_above)
        def _():
            link(up_hbm.at[0, f], 0, 0, f).start()

        @pl.when(has_below)
        def _():
            link(down_hbm.at[1, f], 0, 1, f).start()

    @pl.when(jnp.logical_not(has_above))
    def _():
        for h in range(HOPS):
            for f in range(2):
                from_source(h, f).start()

    @pl.when(jnp.logical_not(has_below))
    def _():
        def clear(t, carry):
            halo[t // 2, 1, lax.rem(t, 2)] = jnp.zeros((2, N, N), BF16)
            return carry

        lax.fori_loop(0, 2 * HOPS, clear, 0)

    greet(near_sem.at[0])

    def propagate(srcs, f):
        fe, ie, fo, io = 0, 1, 2, 3
        n = len(srcs)
        sums, difs = [], []
        for src in srcs:
            re_l, re_r = src[0, :, :H], src[0, :, H:]
            im_l, im_r = src[1, :, :H], src[1, :, H:]
            sums.append(jnp.concatenate([re_l + re_r, im_l + im_r], axis=1))
            difs.append(jnp.concatenate([re_l - re_r, im_l - im_r], axis=1))
        ev = dot(jnp.concatenate(sums, axis=0), tab[ie])
        od = dot(jnp.concatenate(difs, axis=0), tab[io])
        for i in range(n):
            for j, x in enumerate((ev[i * N : (i + 1) * N], od[i * N : (i + 1) * N])):
                cols = slice(j * H, (j + 1) * H)
                u = (x[:H] + x[H:]).astype(BF16)
                v = (x[:H] - x[H:]).astype(BF16)
                s2[i, 0, :H, cols] = u[:, :H]
                s2[i, 0, H:, cols] = u[:, H:]
                s2[i, 1, :H, cols] = v[:, :H]
                s2[i, 1, H:, cols] = v[:, H:]
        for i in range(n):
            for par, t in enumerate((fe, fo)):
                x = dot(tab[t], s2[i, par])
                pr, pi = phase[f, par, 0], phase[f, par, 1]
                re, im = x[:H], x[H:]
                s3[i, par, :H] = (re * pr - im * pi).astype(BF16)
                s3[i, par, H:] = (re * pi + im * pr).astype(BF16)
        for i in range(n):
            e = dot(tab[ie], s3[i, 0])
            o = dot(tab[io], s3[i, 1])
            top = (e + o).astype(BF16)
            bot = (e - o).astype(BF16)
            lo, hi = slice(i * N, i * N + H), slice(i * N + H, i * N + N)
            for j in range(2):
                cols = slice(j * H, (j + 1) * H)
                s4[j, lo, :H] = top[:H, cols]
                s4[j, lo, H:] = top[H:, cols]
                s4[j, hi, :H] = bot[:H, cols]
                s4[j, hi, H:] = bot[H:, cols]
        e = dot(s4[0, : n * N], tab[fe])
        o = dot(s4[1, : n * N], tab[fo])
        sm, df = e + o, e - o
        return [(sm[i * N : (i + 1) * N], df[i * N : (i + 1) * N]) for i in range(n)]

    def screened(x, lev, f, j):
        cols = slice(j * H, (j + 1) * H)
        sr, si = screen[lev, f, 0, :, cols], screen[lev, f, 1, :, cols]
        re, im = x[j][:, :H], x[j][:, H:]
        return (sr * re - si * im, sr * im + si * re)

    def inner_step(f):
        for i, q in enumerate(propagate((local.at[0, f], local.at[1, f]), f)):
            for j in range(2):
                cols = slice(j * H, (j + 1) * H)
                for c, x in enumerate(screened(q, 1 - i, f, j)):
                    inner[1 - i, f, c, :, cols] = x

    rows = N // groups
    scale = 1.0 / math.sqrt(2 * groups)

    def wait_halo(h, k, f):
        @pl.when(linked(k))
        def _():
            link(halo.at[h, k, f], h, 1 - k, f).wait_recv()

        @pl.when(jnp.logical_and(d == 0, k == 0))
        def _():
            from_source(h, f).wait()

    def meet(q, h, k, f, grad):
        for j in range(2):
            cols = slice(j * H, (j + 1) * H)
            r = refl[k, :, cols]
            xs = screened(q, k, f, j)
            g = None
            for c in range(2):
                x, y = xs[c], inner[k, f, c, :, cols]
                t = r * (x - y)
                edge[h, k, f, c, :, cols] = (y + t).astype(BF16)
                local[k, f, c, :, cols] = (x + t).astype(BF16)
                g = x * y if g is None else g + x * y
            if grad == "keep":
                gsum[k, :, cols] = g
            elif grad == "share":
                out = ((gsum[k, :, cols] + g) * scale).astype(BF16)
                for p in range(groups):
                    gsend[k, p, :, cols] = out[p * rows : (p + 1) * rows]

    def send(h, k, f):
        @pl.when(linked(k))
        def _():
            link(edge.at[h, k, f], h + 1, k, f).start()

    mate = s + 1 - 2 * lax.rem(s, 2)

    def over(p, o):
        return lax.rem(p + o, groups)

    peers = [over(mate, 4), over(mate, 2), over(mate, 6), over(s, 4), mate, over(s, 2), over(s, 6)]

    def share(k, i):
        return pltpu.make_async_remote_copy(
            src_ref=gsend.at[k, peers[i]],
            dst_ref=grecv.at[k, i],
            send_sem=gsend_sem.at[k, i],
            recv_sem=grecv_sem.at[k, i],
            device_id={"shot": peers[i]},
            device_id_type=MESH,
        )

    loads[6].wait()
    loads[1].wait()
    loads[2].wait()
    fill_screen(0)
    refl[1] = -refl[1]
    loads[0].wait()
    loads[3].wait()
    loads[4].wait()

    def first(f, carry):
        @pl.when(f == 1)
        def _():
            fill_phase(1)
            fill_screen(1)

        inner_step(f)
        return carry

    lax.fori_loop(0, 2, first, 0)
    pl.semaphore_wait(near_sem.at[0], len(near))
    greet(near_sem.at[1])

    def pair(h, f):
        wait_halo(h, early, f)
        wait_halo(h, late, f)
        return propagate((halo.at[h, late, f], halo.at[h, early, f]), f)

    def middle(t, carry):
        h, f = t // 2, lax.rem(t, 2)
        ql, qe = pair(h, f)
        meet(ql, h, late, f, None)
        send(h, late, f)
        meet(qe, h, early, f, None)
        send(h, early, f)
        inner_step(f)
        return carry

    lax.fori_loop(0, 2 * (HOPS - 1), middle, 0)
    pl.semaphore_wait(near_sem.at[1], len(near))

    end = HOPS - 1
    ql, qe = pair(end, 0)
    meet(ql, end, late, 0, "keep")
    meet(qe, end, early, 0, "keep")

    def final(t, carry):
        k = early + t * (late - early)
        wait_halo(end, k, 1)
        (q,) = propagate((halo.at[end, k, 1],), 1)
        meet(q, end, k, 1, "share")
        for i in range(groups - 1):
            share(k, i).start()
        return carry

    lax.fori_loop(0, 2, final, 0)

    for h in range(HOPS):
        for k in range(2):
            for f in range(2):

                @pl.when(linked(k))
                def _():
                    link(edge.at[0, k, f], h, k, f).wait_send()

    for k in (early, late):
        total = gsend[k, s].astype(F32)
        for i in range(groups - 1):
            share(k, i).wait_recv()
            total = total + grecv[k, i].astype(F32)
        grad_out[k] = total
    for k in range(2):
        for i in range(groups - 1):
            share(k, i).wait_send()


def store(local, edge, grad, down_out, up_out, grad_out, sems):
    last = edge.shape[0] - 1
    pairs = [
        (local.at[0], down_out.at[0]),
        (edge.at[last, 1], down_out.at[1]),
        (edge.at[last, 0], up_out.at[0]),
        (local.at[1], up_out.at[1]),
        (grad, grad_out),
    ]
    copies = [pltpu.make_async_copy(a, b, sems.at[i]) for i, (a, b) in enumerate(pairs)]
    for c in copies:
        c.start()
    for c in copies:
        c.wait()


def solution(mesh):
    groups = mesh.shape["shot"]
    slabs = mesh.shape["depth"]
    rows = N // groups

    def per_device(down_state, up_state, source, reflect, screen_class, screen_values, freq_index):
        table = jnp.asarray(half_tables(), BF16)
        hbm = pl.BlockSpec(memory_space=pltpu.HBM)
        vmem = pl.BlockSpec(memory_space=pltpu.VMEM)
        dma = pltpu.SemaphoreType.DMA
        results = pl.pallas_call(
            lambda *refs: kernel(groups, slabs, *refs),
            out_shape=(
                pltpu.VMEM((2, 2, 2, N, N), BF16),
                pltpu.VMEM((HOPS, 2, 2, 2, N, N), BF16),
                pltpu.VMEM((2, rows, N), F32),
            ),
            in_specs=[hbm] * 8,
            out_specs=(vmem, vmem, vmem),
            scratch_shapes=[
                pltpu.VMEM((4, N, N), BF16),
                pltpu.VMEM((2, N, N), jnp.int32),
                pltpu.VMEM((2, N, N), F32),
                pltpu.VMEM((HOPS, 2, 2, 2, N, N), BF16),
                pltpu.VMEM((2, 2, 2, N, N), F32),
                pltpu.VMEM((2, 2, 2, H, N), F32),
                pltpu.VMEM((2, 2, 2, N, N), F32),
                pltpu.VMEM((2, NCLASS, 8, 128), F32),
                pltpu.VMEM((2, 2, N, N), BF16),
                pltpu.VMEM((2, 2, N, N), BF16),
                pltpu.VMEM((2, 2 * N, N), BF16),
                pltpu.VMEM((2, N, N), F32),
                pltpu.VMEM((2, groups, rows, N), BF16),
                pltpu.VMEM((2, groups - 1, rows, N), BF16),
                pltpu.SMEM((NCLASS,), F32),
                pltpu.SMEM((2,), jnp.int32),
                dma((7,)),
                dma((HOPS, 2)),
                dma((HOPS, 2, 2)),
                dma((HOPS, 2, 2)),
                dma((2, groups - 1)),
                dma((2, groups - 1)),
                pltpu.SemaphoreType.REGULAR((2,)),
            ],
            compiler_params=pltpu.CompilerParams(
                collective_id=0, has_side_effects=True, vmem_limit_bytes=40 * 1024 * 1024
            ),
        )(
            *(
                pltpu.with_memory_space_constraint(x, pltpu.HBM)
                for x in (
                    screen_values,
                    freq_index,
                    down_state,
                    up_state,
                    source,
                    reflect,
                    screen_class,
                    table,
                )
            ),
        )
        return pl.pallas_call(
            store,
            out_shape=[
                pltpu.HBM(down_state.shape, BF16),
                pltpu.HBM(up_state.shape, BF16),
                pltpu.HBM((2, rows, N), F32),
            ],
            in_specs=[vmem] * 3,
            out_specs=[hbm] * 3,
            scratch_shapes=[dma((5,))],
            compiler_params=pltpu.CompilerParams(vmem_limit_bytes=1024 * 1024),
        )(*(pltpu.with_memory_space_constraint(x, pltpu.VMEM) for x in results))

    return jax.shard_map(
        per_device,
        mesh=mesh,
        in_specs=(
            P("depth", "shot", None, None, None),
            P("depth", "shot", None, None, None),
            P("shot", None, None, None),
            P("depth", None, None),
            P("depth", None, None),
            P(),
            P("shot"),
        ),
        out_specs=(
            P("depth", "shot", None, None, None),
            P("depth", "shot", None, None, None),
            P("depth", "shot", None),
        ),
        check_vma=False,
    )
```

```python
import math

import jax
import jax.numpy as jnp
import numpy as np
from jax import lax
from jax.experimental import pallas as pl
from jax.experimental.pallas import tpu as pltpu
from jax.sharding import PartitionSpec as P

HOPS = 3
NCLASS = 16
NFREQ = 128
N = 256
H = N // 2
MESH = pl.DeviceIdType.MESH
BF16 = jnp.bfloat16
F32 = jnp.float32
COS_COEFS = [(-1.0) ** k / math.factorial(2 * k) for k in range(10)]
SIN_COEFS = [(-1.0) ** k / math.factorial(2 * k + 1) for k in range(10)]


def half_tables():
    row = np.arange(H)[:, None]
    col = np.arange(H)[None, :]
    mats = []
    for parity in (0, 1):
        angle = (2.0 * math.pi / N) * (((2 * row + parity) * col) % N).astype(np.float64)
        cos, sin = np.cos(angle), np.sin(angle)
        fwd = np.block([[cos, sin], [-sin, cos]])
        mats.append(fwd)
        mats.append(fwd.T)
    return np.stack(mats).astype(np.float32)


def poly(coefs, q):
    acc = jnp.full_like(q, coefs[-1])
    for c in coefs[-2::-1]:
        acc = acc * q + c
    return acc


def dot(a, b):
    return jnp.dot(a, b, preferred_element_type=F32)


def kernel(
    groups,
    slabs,
    values_hbm,
    freq_hbm,
    down_hbm,
    up_hbm,
    source_hbm,
    reflect_hbm,
    class_hbm,
    table_hbm,
    local,
    edge,
    grad_out,
    tab,
    classes,
    refl,
    halo,
    inner,
    phase,
    screen,
    lut,
    s2,
    s3,
    s4,
    gsum,
    final_x,
    gsend,
    grecv,
    screen_values,
    freq_index,
    load_sem,
    src_sem,
    send_sem,
    recv_sem,
    gsend_sem,
    grecv_sem,
    near_sem,
):
    d = lax.axis_index("depth")
    s = lax.axis_index("shot")
    has_above = d > 0
    has_below = d < slabs - 1

    loads = [
        pltpu.make_async_copy(table_hbm, tab, load_sem.at[0]),
        pltpu.make_async_copy(class_hbm, classes, load_sem.at[1]),
        pltpu.make_async_copy(reflect_hbm, refl, load_sem.at[2]),
        pltpu.make_async_copy(down_hbm.at[0], local.at[0], load_sem.at[3]),
        pltpu.make_async_copy(up_hbm.at[1], local.at[1], load_sem.at[4]),
        pltpu.make_async_copy(freq_hbm, freq_index, load_sem.at[5]),
        pltpu.make_async_copy(values_hbm, screen_values, load_sem.at[6]),
    ]
    near = [
        lax.rem(s + 2, groups),
        lax.rem(s + groups - 2, groups),
        s + 1 - 2 * lax.rem(s, 2),
    ]

    def greet(sem):
        for peer in near:
            pl.semaphore_signal(sem, inc=1, device_id={"shot": peer}, device_id_type=MESH)

    barrier = pltpu.get_barrier_semaphore()

    @pl.when(has_above)
    def _():
        pl.semaphore_signal(barrier, inc=1, device_id={"depth": d - 1}, device_id_type=MESH)

    @pl.when(has_below)
    def _():
        pl.semaphore_signal(barrier, inc=1, device_id={"depth": d + 1}, device_id_type=MESH)

    greet(barrier)
    for c in loads[::-1]:
        c.start()

    def link(src, h, k, f):
        return pltpu.make_async_remote_copy(
            src_ref=src,
            dst_ref=halo.at[h, 1 - k, f],
            send_sem=send_sem.at[h, k, f],
            recv_sem=recv_sem.at[h, 1 - k, f],
            device_id={"depth": lax.rem(d + 2 * k + slabs - 1, slabs)},
            device_id_type=MESH,
        )

    def linked(k):
        peer = d + 2 * k - 1
        return jnp.logical_and(peer >= 0, peer < slabs)

    def from_source(h, f):
        return pltpu.make_async_copy(source_hbm.at[f], halo.at[h, 0, f], src_sem.at[h, f])

    late = lax.rem(d, 2)
    early = 1 - late

    def fill_phase(t, carry):
        r0 = pl.multiple_of(t * 8, 8)
        row = lax.broadcasted_iota(jnp.int32, (8, N), 0) + r0
        lane = lax.broadcasted_iota(jnp.int32, (8, N), 1)
        ym = jnp.where(lane < H, 2 * lane, 2 * (lane - H) + 1)
        ym = jnp.where(ym >= H, ym - N, ym)
        ky = (2.0 * math.pi / N) * ym.astype(F32)
        for par in range(2):
            xm = 2 * row + par
            xm = jnp.where(xm >= H, xm - N, xm)
            kx = (2.0 * math.pi / N) * xm.astype(F32)
            k2 = kx * kx + ky * ky
            for f in range(2):
                q = kwave[f] * kwave[f] - k2
                root = jnp.sqrt(jnp.abs(q))
                qp = jnp.maximum(q, 0.0)
                damp = jnp.where(q < 0.0, jnp.exp(-root), 1.0) * (1.0 / (N * N))
                sin = jnp.where(q > 0.0, root, 0.0) * poly(SIN_COEFS, qp)
                phase[f, par, 0, pl.ds(r0, 8), :] = damp * poly(COS_COEFS, qp)
                phase[f, par, 1, pl.ds(r0, 8), :] = damp * sin
        return carry

    def fill_screen(f):
        k0 = 0.95 * math.pi * (freq_index[f].astype(F32) + 1.0) / NFREQ
        for c in range(NCLASS):
            ang = jnp.full((8, 128), k0 * screen_values[c], F32)
            q = ang * ang
            lut[0, c] = poly(COS_COEFS, q)
            lut[1, c] = ang * poly(SIN_COEFS, q)

        def rows(t, carry):
            lev = t // (N // 32)
            r0 = pl.multiple_of(lax.rem(t, N // 32) * 32, 32)
            tables = [[lut[k, c] for c in range(NCLASS)] for k in range(2)]
            for i in range(4):
                for j in range(2):
                    here = (pl.ds(r0 + 8 * i, 8), pl.ds(j * H, H))
                    cls = classes[lev, *here]
                    bits = [(cls & (1 << b)) != 0 for b in range(4)]
                    for k in range(2):
                        vals = tables[k]
                        for bit in bits:
                            vals = [
                                jnp.where(bit, vals[2 * m + 1], vals[2 * m])
                                for m in range(len(vals) // 2)
                            ]
                        screen[lev, f, k, *here] = vals[0]
            return carry

        lax.fori_loop(0, 2 * N // 32, rows, 0)

    loads[5].wait()
    kwave = [0.95 * math.pi * (freq_index[f].astype(F32) + 1.0) / NFREQ for f in range(2)]
    lax.fori_loop(0, H // 8, fill_phase, 0)
    pl.semaphore_wait(
        barrier, len(near) + has_above.astype(jnp.int32) + has_below.astype(jnp.int32)
    )

    for f in range(2):

        @pl.when(has_above)
        def _():
            link(up_hbm.at[0, f], 0, 0, f).start()

        @pl.when(has_below)
        def _():
            link(down_hbm.at[1, f], 0, 1, f).start()

    @pl.when(jnp.logical_not(has_above))
    def _():
        for h in range(HOPS):
            for f in range(2):
                from_source(h, f).start()

    @pl.when(jnp.logical_not(has_below))
    def _():
        def clear(t, carry):
            halo[t // 2, 1, lax.rem(t, 2)] = jnp.zeros((2, N, N), BF16)
            return carry

        lax.fori_loop(0, 2 * HOPS, clear, 0)

    greet(near_sem.at[0])

    def propagate(srcs, f):
        fe, ie, fo, io = 0, 1, 2, 3
        n = len(srcs)
        sums, difs = [], []
        for src in srcs:
            re_l, re_r = src[0, :, :H], src[0, :, H:]
            im_l, im_r = src[1, :, :H], src[1, :, H:]
            sums.append(jnp.concatenate([re_l + re_r, im_l + im_r], axis=1))
            difs.append(jnp.concatenate([re_l - re_r, im_l - im_r], axis=1))
        ev = dot(jnp.concatenate(sums, axis=0), tab[ie])
        od = dot(jnp.concatenate(difs, axis=0), tab[io])
        for i in range(n):
            for j, x in enumerate((ev[i * N : (i + 1) * N], od[i * N : (i + 1) * N])):
                cols = slice(j * H, (j + 1) * H)
                u = (x[:H] + x[H:]).astype(BF16)
                v = (x[:H] - x[H:]).astype(BF16)
                s2[i, 0, :H, cols] = u[:, :H]
                s2[i, 0, H:, cols] = u[:, H:]
                s2[i, 1, :H, cols] = v[:, :H]
                s2[i, 1, H:, cols] = v[:, H:]
        for i in range(n):
            for par, t in enumerate((fe, fo)):
                x = dot(tab[t], s2[i, par])
                pr, pi = phase[f, par, 0], phase[f, par, 1]
                re, im = x[:H], x[H:]
                s3[i, par, :H] = (re * pr - im * pi).astype(BF16)
                s3[i, par, H:] = (re * pi + im * pr).astype(BF16)
        for i in range(n):
            e = dot(tab[ie], s3[i, 0])
            o = dot(tab[io], s3[i, 1])
            top = (e + o).astype(BF16)
            bot = (e - o).astype(BF16)
            lo, hi = slice(i * N, i * N + H), slice(i * N + H, i * N + N)
            for j in range(2):
                cols = slice(j * H, (j + 1) * H)
                s4[j, lo, :H] = top[:H, cols]
                s4[j, lo, H:] = top[H:, cols]
                s4[j, hi, :H] = bot[:H, cols]
                s4[j, hi, H:] = bot[H:, cols]
        e = dot(s4[0, : n * N], tab[fe])
        o = dot(s4[1, : n * N], tab[fo])
        sm, df = e + o, e - o
        return [(sm[i * N : (i + 1) * N], df[i * N : (i + 1) * N]) for i in range(n)]

    def screened(x, lev, f, j):
        cols = slice(j * H, (j + 1) * H)
        sr, si = screen[lev, f, 0, :, cols], screen[lev, f, 1, :, cols]
        re, im = x[j][:, :H], x[j][:, H:]
        return (sr * re - si * im, sr * im + si * re)

    def inner_step(f):
        for i, q in enumerate(propagate((local.at[0, f], local.at[1, f]), f)):
            for j in range(2):
                cols = slice(j * H, (j + 1) * H)
                for c, x in enumerate(screened(q, 1 - i, f, j)):
                    inner[1 - i, f, c, :, cols] = x

    rows = N // groups
    scale = 1.0 / math.sqrt(2 * groups)

    def wait_halo(h, k, f):
        @pl.when(linked(k))
        def _():
            link(halo.at[h, k, f], h, 1 - k, f).wait_recv()

        @pl.when(jnp.logical_and(d == 0, k == 0))
        def _():
            from_source(h, f).wait()

    def meet(q, h, k, f, keep):
        for j in range(2):
            cols = slice(j * H, (j + 1) * H)
            r = refl[k, :, cols]
            xs = screened(q, k, f, j)
            g = None
            for c in range(2):
                x, y = xs[c], inner[k, f, c, :, cols]
                t = r * (x - y)
                edge[h, k, f, c, :, cols] = (y + t).astype(BF16)
                local[k, f, c, :, cols] = (x + t).astype(BF16)
                g = x * y if g is None else g + x * y
            if keep:
                gsum[k, :, cols] = g

    def meet_last(q, h, k, f):
        for j in range(2):
            cols = slice(j * H, (j + 1) * H)
            re, im = screened(q, k, f, j)
            final_x[0, :, cols] = re
            final_x[1, :, cols] = im
            g = re * inner[k, f, 0, :, cols] + im * inner[k, f, 1, :, cols]
            out = ((gsum[k, :, cols] + g) * scale).astype(BF16)
            for p in range(groups):
                gsend[k, p, :, cols] = out[p * rows : (p + 1) * rows]
        for i in range(groups - 1):
            share(k, i).start()
        for c in range(2):
            x, y = final_x[c], inner[k, f, c]
            t = refl[k] * (x - y)
            edge[h, k, f, c] = (y + t).astype(BF16)
            local[k, f, c] = (x + t).astype(BF16)

    def send(h, k, f):
        @pl.when(linked(k))
        def _():
            link(edge.at[h, k, f], h + 1, k, f).start()

    mate = s + 1 - 2 * lax.rem(s, 2)

    def over(p, o):
        return lax.rem(p + o, groups)

    peers = [over(mate, 4), over(mate, 2), over(mate, 6), over(s, 4), mate, over(s, 2), over(s, 6)]

    def share(k, i):
        return pltpu.make_async_remote_copy(
            src_ref=gsend.at[k, peers[i]],
            dst_ref=grecv.at[k, i],
            send_sem=gsend_sem.at[k, i],
            recv_sem=grecv_sem.at[k, i],
            device_id={"shot": peers[i]},
            device_id_type=MESH,
        )

    loads[6].wait()
    loads[1].wait()
    loads[2].wait()
    fill_screen(0)
    refl[1] = -refl[1]
    loads[0].wait()
    loads[3].wait()
    loads[4].wait()

    def first(f, carry):
        @pl.when(f == 1)
        def _():
            fill_screen(1)

        inner_step(f)
        return carry

    lax.fori_loop(0, 2, first, 0)
    pl.semaphore_wait(near_sem.at[0], len(near))
    greet(near_sem.at[1])

    def pair(h, f):
        wait_halo(h, early, f)
        wait_halo(h, late, f)
        return propagate((halo.at[h, late, f], halo.at[h, early, f]), f)

    def middle(t, carry):
        h, f = t // 2, lax.rem(t, 2)
        ql, qe = pair(h, f)
        meet(ql, h, late, f, False)
        send(h, late, f)
        meet(qe, h, early, f, False)
        send(h, early, f)
        inner_step(f)
        return carry

    lax.fori_loop(0, 2 * (HOPS - 1), middle, 0)
    pl.semaphore_wait(near_sem.at[1], len(near))

    end = HOPS - 1
    ql, qe = pair(end, 0)
    meet(ql, end, late, 0, True)
    meet(qe, end, early, 0, True)

    def final(t, carry):
        k = early + t * (late - early)
        wait_halo(end, k, 1)
        (q,) = propagate((halo.at[end, k, 1],), 1)
        meet_last(q, end, k, 1)
        return carry

    lax.fori_loop(0, 2, final, 0)

    for h in range(HOPS):
        for k in range(2):
            for f in range(2):

                @pl.when(linked(k))
                def _():
                    link(edge.at[0, k, f], h, k, f).wait_send()

    for k in (early, late):
        total = gsend[k, s].astype(F32)
        for i in range(groups - 1):
            share(k, i).wait_recv()
            total = total + grecv[k, i].astype(F32)
        grad_out[k] = total
    for k in range(2):
        for i in range(groups - 1):
            share(k, i).wait_send()


def store(local, edge, grad, down_out, up_out, grad_out, sems):
    last = edge.shape[0] - 1
    pairs = [
        (local.at[0], down_out.at[0]),
        (edge.at[last, 1], down_out.at[1]),
        (edge.at[last, 0], up_out.at[0]),
        (local.at[1], up_out.at[1]),
        (grad, grad_out),
    ]
    copies = [pltpu.make_async_copy(a, b, sems.at[i]) for i, (a, b) in enumerate(pairs)]
    for c in copies:
        c.start()
    for c in copies:
        c.wait()


def solution(mesh):
    groups = mesh.shape["shot"]
    slabs = mesh.shape["depth"]
    rows = N // groups

    def per_device(down_state, up_state, source, reflect, screen_class, screen_values, freq_index):
        table = jnp.asarray(half_tables(), BF16)
        hbm = pl.BlockSpec(memory_space=pltpu.HBM)
        vmem = pl.BlockSpec(memory_space=pltpu.VMEM)
        dma = pltpu.SemaphoreType.DMA
        results = pl.pallas_call(
            lambda *refs: kernel(groups, slabs, *refs),
            out_shape=(
                pltpu.VMEM((2, 2, 2, N, N), BF16),
                pltpu.VMEM((HOPS, 2, 2, 2, N, N), BF16),
                pltpu.VMEM((2, rows, N), F32),
            ),
            in_specs=[hbm] * 8,
            out_specs=(vmem, vmem, vmem),
            scratch_shapes=[
                pltpu.VMEM((4, N, N), BF16),
                pltpu.VMEM((2, N, N), jnp.int32),
                pltpu.VMEM((2, N, N), F32),
                pltpu.VMEM((HOPS, 2, 2, 2, N, N), BF16),
                pltpu.VMEM((2, 2, 2, N, N), F32),
                pltpu.VMEM((2, 2, 2, H, N), F32),
                pltpu.VMEM((2, 2, 2, N, N), F32),
                pltpu.VMEM((2, NCLASS, 8, 128), F32),
                pltpu.VMEM((2, 2, N, N), BF16),
                pltpu.VMEM((2, 2, N, N), BF16),
                pltpu.VMEM((2, 2 * N, N), BF16),
                pltpu.VMEM((2, N, N), F32),
                pltpu.VMEM((2, N, N), F32),
                pltpu.VMEM((2, groups, rows, N), BF16),
                pltpu.VMEM((2, groups - 1, rows, N), BF16),
                pltpu.SMEM((NCLASS,), F32),
                pltpu.SMEM((2,), jnp.int32),
                dma((7,)),
                dma((HOPS, 2)),
                dma((HOPS, 2, 2)),
                dma((HOPS, 2, 2)),
                dma((2, groups - 1)),
                dma((2, groups - 1)),
                pltpu.SemaphoreType.REGULAR((2,)),
            ],
            compiler_params=pltpu.CompilerParams(
                collective_id=0, has_side_effects=True, vmem_limit_bytes=40 * 1024 * 1024
            ),
        )(
            *(
                pltpu.with_memory_space_constraint(x, pltpu.HBM)
                for x in (
                    screen_values,
                    freq_index,
                    down_state,
                    up_state,
                    source,
                    reflect,
                    screen_class,
                    table,
                )
            ),
        )
        return pl.pallas_call(
            store,
            out_shape=[
                pltpu.HBM(down_state.shape, BF16),
                pltpu.HBM(up_state.shape, BF16),
                pltpu.HBM((2, rows, N), F32),
            ],
            in_specs=[vmem] * 3,
            out_specs=[hbm] * 3,
            scratch_shapes=[dma((5,))],
            compiler_params=pltpu.CompilerParams(vmem_limit_bytes=1024 * 1024),
        )(*(pltpu.with_memory_space_constraint(x, pltpu.VMEM) for x in results))

    return jax.shard_map(
        per_device,
        mesh=mesh,
        in_specs=(
            P("depth", "shot", None, None, None),
            P("depth", "shot", None, None, None),
            P("shot", None, None, None),
            P("depth", None, None),
            P("depth", None, None),
            P(),
            P("shot"),
        ),
        out_specs=(
            P("depth", "shot", None, None, None),
            P("depth", "shot", None, None, None),
            P("depth", "shot", None),
        ),
        check_vma=False,
    )
```

```python
import math

import jax
import jax.numpy as jnp
import numpy as np
from jax import lax
from jax.experimental import pallas as pl
from jax.experimental.pallas import tpu as pltpu
from jax.sharding import PartitionSpec as P

HOPS = 3
NCLASS = 16
NFREQ = 128
N = 256
H = N // 2
MESH = pl.DeviceIdType.MESH
BF16 = jnp.bfloat16
F32 = jnp.float32
COS_COEFS = [(-1.0) ** k / math.factorial(2 * k) for k in range(10)]
SIN_COEFS = [(-1.0) ** k / math.factorial(2 * k + 1) for k in range(10)]


def half_tables():
    row = np.arange(H)[:, None]
    col = np.arange(H)[None, :]
    mats = []
    for parity in (0, 1):
        angle = (2.0 * math.pi / N) * (((2 * row + parity) * col) % N).astype(np.float64)
        cos, sin = np.cos(angle), np.sin(angle)
        fwd = np.block([[cos, sin], [-sin, cos]])
        mats.append(fwd)
        mats.append(fwd.T)
    return np.stack(mats).astype(np.float32)


def poly(coefs, q):
    acc = jnp.full_like(q, coefs[-1])
    for c in coefs[-2::-1]:
        acc = acc * q + c
    return acc


def dot(a, b):
    return jnp.dot(a, b, preferred_element_type=F32)


def kernel(
    groups,
    slabs,
    values_hbm,
    freq_hbm,
    down_hbm,
    up_hbm,
    source_hbm,
    reflect_hbm,
    class_hbm,
    table_hbm,
    local,
    edge,
    grad_out,
    tab,
    classes,
    refl,
    halo,
    inner,
    phase,
    screen,
    lut,
    s2,
    s3,
    s4,
    gsum,
    final_x,
    gsend,
    grecv,
    screen_values,
    freq_index,
    load_sem,
    src_sem,
    send_sem,
    recv_sem,
    gsend_sem,
    grecv_sem,
    near_sem,
):
    d = lax.axis_index("depth")
    s = lax.axis_index("shot")
    has_above = d > 0
    has_below = d < slabs - 1

    loads = [
        pltpu.make_async_copy(table_hbm, tab, load_sem.at[0]),
        pltpu.make_async_copy(class_hbm, classes, load_sem.at[1]),
        pltpu.make_async_copy(reflect_hbm, refl, load_sem.at[2]),
        pltpu.make_async_copy(down_hbm.at[0], local.at[0], load_sem.at[3]),
        pltpu.make_async_copy(up_hbm.at[1], local.at[1], load_sem.at[4]),
        pltpu.make_async_copy(freq_hbm, freq_index, load_sem.at[5]),
        pltpu.make_async_copy(values_hbm, screen_values, load_sem.at[6]),
    ]
    near = [
        lax.rem(s + 2, groups),
        lax.rem(s + groups - 2, groups),
        s + 1 - 2 * lax.rem(s, 2),
    ]

    def greet(sem):
        for peer in near:
            pl.semaphore_signal(sem, inc=1, device_id={"shot": peer}, device_id_type=MESH)

    barrier = pltpu.get_barrier_semaphore()

    @pl.when(has_above)
    def _():
        pl.semaphore_signal(barrier, inc=1, device_id={"depth": d - 1}, device_id_type=MESH)

    @pl.when(has_below)
    def _():
        pl.semaphore_signal(barrier, inc=1, device_id={"depth": d + 1}, device_id_type=MESH)

    greet(barrier)
    for c in loads[::-1]:
        c.start()

    def link(src, h, k, f):
        return pltpu.make_async_remote_copy(
            src_ref=src,
            dst_ref=halo.at[h, 1 - k, f],
            send_sem=send_sem.at[h, k, f],
            recv_sem=recv_sem.at[h, 1 - k, f],
            device_id={"depth": lax.rem(d + 2 * k + slabs - 1, slabs)},
            device_id_type=MESH,
        )

    def linked(k):
        peer = d + 2 * k - 1
        return jnp.logical_and(peer >= 0, peer < slabs)

    def from_source(h, f):
        return pltpu.make_async_copy(source_hbm.at[f], halo.at[h, 0, f], src_sem.at[h, f])

    turn = slabs // 2
    holds = d == turn + 1
    late = lax.rem(d, 2)
    early = 1 - late

    def fill_phase(t, carry):
        r0 = pl.multiple_of(t * 8, 8)
        row = lax.broadcasted_iota(jnp.int32, (8, N), 0) + r0
        lane = lax.broadcasted_iota(jnp.int32, (8, N), 1)
        ym = jnp.where(lane < H, 2 * lane, 2 * (lane - H) + 1)
        ym = jnp.where(ym >= H, ym - N, ym)
        ky = (2.0 * math.pi / N) * ym.astype(F32)
        for par in range(2):
            xm = 2 * row + par
            xm = jnp.where(xm >= H, xm - N, xm)
            kx = (2.0 * math.pi / N) * xm.astype(F32)
            k2 = kx * kx + ky * ky
            for f in range(2):
                q = kwave[f] * kwave[f] - k2
                root = jnp.sqrt(jnp.abs(q))
                qp = jnp.maximum(q, 0.0)
                damp = jnp.where(q < 0.0, jnp.exp(-root), 1.0) * (1.0 / (N * N))
                sin = jnp.where(q > 0.0, root, 0.0) * poly(SIN_COEFS, qp)
                phase[f, par, 0, pl.ds(r0, 8), :] = damp * poly(COS_COEFS, qp)
                phase[f, par, 1, pl.ds(r0, 8), :] = damp * sin
        return carry

    def fill_screen(f):
        k0 = 0.95 * math.pi * (freq_index[f].astype(F32) + 1.0) / NFREQ
        for c in range(NCLASS):
            ang = jnp.full((8, 128), k0 * screen_values[c], F32)
            q = ang * ang
            lut[0, c] = poly(COS_COEFS, q)
            lut[1, c] = ang * poly(SIN_COEFS, q)

        def rows(t, carry):
            lev = t // (N // 32)
            r0 = pl.multiple_of(lax.rem(t, N // 32) * 32, 32)
            tables = [[lut[k, c] for c in range(NCLASS)] for k in range(2)]
            for i in range(4):
                for j in range(2):
                    here = (pl.ds(r0 + 8 * i, 8), pl.ds(j * H, H))
                    cls = classes[lev, *here]
                    bits = [(cls & (1 << b)) != 0 for b in range(4)]
                    for k in range(2):
                        vals = tables[k]
                        for bit in bits:
                            vals = [
                                jnp.where(bit, vals[2 * m + 1], vals[2 * m])
                                for m in range(len(vals) // 2)
                            ]
                        screen[lev, f, k, *here] = vals[0]
            return carry

        lax.fori_loop(0, 2 * N // 32, rows, 0)

    loads[5].wait()
    kwave = [0.95 * math.pi * (freq_index[f].astype(F32) + 1.0) / NFREQ for f in range(2)]
    lax.fori_loop(0, H // 8, fill_phase, 0)
    pl.semaphore_wait(
        barrier, len(near) + has_above.astype(jnp.int32) + has_below.astype(jnp.int32)
    )

    for f in range(2):

        @pl.when(has_above)
        def _():
            link(up_hbm.at[0, f], 0, 0, f).start()

        @pl.when(has_below)
        def _():
            link(down_hbm.at[1, f], 0, 1, f).start()

    @pl.when(jnp.logical_not(has_above))
    def _():
        for h in range(HOPS):
            for f in range(2):
                from_source(h, f).start()

    @pl.when(jnp.logical_not(has_below))
    def _():
        def clear(t, carry):
            halo[t // 2, 1, lax.rem(t, 2)] = jnp.zeros((2, N, N), BF16)
            return carry

        lax.fori_loop(0, 2 * HOPS, clear, 0)

    greet(near_sem.at[0])

    def propagate(srcs, f):
        fe, ie, fo, io = 0, 1, 2, 3
        n = len(srcs)
        sums, difs = [], []
        for src in srcs:
            re_l, re_r = src[0, :, :H], src[0, :, H:]
            im_l, im_r = src[1, :, :H], src[1, :, H:]
            sums.append(jnp.concatenate([re_l + re_r, im_l + im_r], axis=1))
            difs.append(jnp.concatenate([re_l - re_r, im_l - im_r], axis=1))
        ev = dot(jnp.concatenate(sums, axis=0), tab[ie])
        od = dot(jnp.concatenate(difs, axis=0), tab[io])
        for i in range(n):
            for j, x in enumerate((ev[i * N : (i + 1) * N], od[i * N : (i + 1) * N])):
                cols = slice(j * H, (j + 1) * H)
                u = (x[:H] + x[H:]).astype(BF16)
                v = (x[:H] - x[H:]).astype(BF16)
                s2[i, 0, :H, cols] = u[:, :H]
                s2[i, 0, H:, cols] = u[:, H:]
                s2[i, 1, :H, cols] = v[:, :H]
                s2[i, 1, H:, cols] = v[:, H:]
        for i in range(n):
            for par, t in enumerate((fe, fo)):
                x = dot(tab[t], s2[i, par])
                pr, pi = phase[f, par, 0], phase[f, par, 1]
                re, im = x[:H], x[H:]
                s3[i, par, :H] = (re * pr - im * pi).astype(BF16)
                s3[i, par, H:] = (re * pi + im * pr).astype(BF16)
        for i in range(n):
            e = dot(tab[ie], s3[i, 0])
            o = dot(tab[io], s3[i, 1])
            top = (e + o).astype(BF16)
            bot = (e - o).astype(BF16)
            lo, hi = slice(i * N, i * N + H), slice(i * N + H, i * N + N)
            for j in range(2):
                cols = slice(j * H, (j + 1) * H)
                s4[j, lo, :H] = top[:H, cols]
                s4[j, lo, H:] = top[H:, cols]
                s4[j, hi, :H] = bot[:H, cols]
                s4[j, hi, H:] = bot[H:, cols]
        e = dot(s4[0, : n * N], tab[fe])
        o = dot(s4[1, : n * N], tab[fo])
        sm, df = e + o, e - o
        return [(sm[i * N : (i + 1) * N], df[i * N : (i + 1) * N]) for i in range(n)]

    def screened(x, lev, f, j):
        cols = slice(j * H, (j + 1) * H)
        sr, si = screen[lev, f, 0, :, cols], screen[lev, f, 1, :, cols]
        re, im = x[j][:, :H], x[j][:, H:]
        return (sr * re - si * im, sr * im + si * re)

    def inner_step(f):
        for i, q in enumerate(propagate((local.at[0, f], local.at[1, f]), f)):
            for j in range(2):
                cols = slice(j * H, (j + 1) * H)
                for c, x in enumerate(screened(q, 1 - i, f, j)):
                    inner[1 - i, f, c, :, cols] = x

    rows = N // groups
    scale = 1.0 / math.sqrt(2 * groups)

    def wait_halo(h, k, f):
        @pl.when(linked(k))
        def _():
            link(halo.at[h, k, f], h, 1 - k, f).wait_recv()

        @pl.when(jnp.logical_and(d == 0, k == 0))
        def _():
            from_source(h, f).wait()

    def meet(q, h, k, f, keep):
        for j in range(2):
            cols = slice(j * H, (j + 1) * H)
            r = refl[k, :, cols]
            xs = screened(q, k, f, j)
            g = None
            for c in range(2):
                x, y = xs[c], inner[k, f, c, :, cols]
                t = r * (x - y)
                edge[h, k, f, c, :, cols] = (y + t).astype(BF16)
                local[k, f, c, :, cols] = (x + t).astype(BF16)
                g = x * y if g is None else g + x * y
            if keep:
                gsum[k, :, cols] = g

    def meet_last(q, h, k, f):
        for j in range(2):
            cols = slice(j * H, (j + 1) * H)
            re, im = screened(q, k, f, j)
            final_x[0, :, cols] = re
            final_x[1, :, cols] = im
            g = re * inner[k, f, 0, :, cols] + im * inner[k, f, 1, :, cols]
            out = ((gsum[k, :, cols] + g) * scale).astype(BF16)
            for p in range(groups):
                gsend[k, p, :, cols] = out[p * rows : (p + 1) * rows]

        @pl.when(jnp.logical_not(holds))
        def _():
            for i in range(groups - 1):
                share(k, i).start()

        for c in range(2):
            x, y = final_x[c], inner[k, f, c]
            t = refl[k] * (x - y)
            edge[h, k, f, c] = (y + t).astype(BF16)
            local[k, f, c] = (x + t).astype(BF16)

    def send(h, k, f):
        @pl.when(linked(k))
        def _():
            link(edge.at[h, k, f], h + 1, k, f).start()

    mate = s + 1 - 2 * lax.rem(s, 2)

    def over(p, o):
        return lax.rem(p + o, groups)

    peers = [over(mate, 4), over(mate, 2), over(mate, 6), over(s, 4), mate, over(s, 2), over(s, 6)]

    def share(k, i):
        return pltpu.make_async_remote_copy(
            src_ref=gsend.at[k, peers[i]],
            dst_ref=grecv.at[k, i],
            send_sem=gsend_sem.at[k, i],
            recv_sem=grecv_sem.at[k, i],
            device_id={"shot": peers[i]},
            device_id_type=MESH,
        )

    loads[6].wait()
    loads[1].wait()
    loads[2].wait()
    fill_screen(0)
    refl[1] = -refl[1]
    loads[0].wait()
    loads[3].wait()
    loads[4].wait()

    def first(f, carry):
        @pl.when(f == 1)
        def _():
            fill_screen(1)

        inner_step(f)
        return carry

    lax.fori_loop(0, 2, first, 0)
    pl.semaphore_wait(near_sem.at[0], len(near))
    greet(near_sem.at[1])

    def pair(h, f):
        wait_halo(h, early, f)
        wait_halo(h, late, f)
        return propagate((halo.at[h, late, f], halo.at[h, early, f]), f)

    def middle(t, carry):
        h, f = t // 2, lax.rem(t, 2)
        ql, qe = pair(h, f)
        meet(ql, h, late, f, False)
        send(h, late, f)
        meet(qe, h, early, f, False)
        send(h, early, f)
        inner_step(f)
        return carry

    lax.fori_loop(0, 2 * (HOPS - 1), middle, 0)
    pl.semaphore_wait(near_sem.at[1], len(near))

    end = HOPS - 1
    ql, qe = pair(end, 0)
    meet(ql, end, late, 0, True)
    meet(qe, end, early, 0, True)

    def final(t, carry):
        k = early + t * (late - early)
        wait_halo(end, k, 1)

        @pl.when(jnp.logical_and(d == turn, t == 1))
        def _():
            pl.semaphore_signal(
                near_sem.at[2], inc=1, device_id={"depth": d + 1}, device_id_type=MESH
            )

        (q,) = propagate((halo.at[end, k, 1],), 1)
        meet_last(q, end, k, 1)
        return carry

    lax.fori_loop(0, 2, final, 0)

    @pl.when(holds)
    def _():
        pl.semaphore_wait(near_sem.at[2], 1)
        for k in range(2):
            for i in range(groups - 1):
                share(k, i).start()

    for h in range(HOPS):
        for k in range(2):
            for f in range(2):

                @pl.when(linked(k))
                def _():
                    link(edge.at[0, k, f], h, k, f).wait_send()

    for k in (early, late):
        total = gsend[k, s].astype(F32)
        for i in range(groups - 1):
            share(k, i).wait_recv()
            total = total + grecv[k, i].astype(F32)
        grad_out[k] = total
    for k in range(2):
        for i in range(groups - 1):
            share(k, i).wait_send()


def store(local, edge, grad, down_out, up_out, grad_out, sems):
    last = edge.shape[0] - 1
    pairs = [
        (local.at[0], down_out.at[0]),
        (edge.at[last, 1], down_out.at[1]),
        (edge.at[last, 0], up_out.at[0]),
        (local.at[1], up_out.at[1]),
        (grad, grad_out),
    ]
    copies = [pltpu.make_async_copy(a, b, sems.at[i]) for i, (a, b) in enumerate(pairs)]
    for c in copies:
        c.start()
    for c in copies:
        c.wait()


def solution(mesh):
    groups = mesh.shape["shot"]
    slabs = mesh.shape["depth"]
    rows = N // groups

    def per_device(down_state, up_state, source, reflect, screen_class, screen_values, freq_index):
        table = jnp.asarray(half_tables(), BF16)
        hbm = pl.BlockSpec(memory_space=pltpu.HBM)
        vmem = pl.BlockSpec(memory_space=pltpu.VMEM)
        dma = pltpu.SemaphoreType.DMA
        results = pl.pallas_call(
            lambda *refs: kernel(groups, slabs, *refs),
            out_shape=(
                pltpu.VMEM((2, 2, 2, N, N), BF16),
                pltpu.VMEM((HOPS, 2, 2, 2, N, N), BF16),
                pltpu.VMEM((2, rows, N), F32),
            ),
            in_specs=[hbm] * 8,
            out_specs=(vmem, vmem, vmem),
            scratch_shapes=[
                pltpu.VMEM((4, N, N), BF16),
                pltpu.VMEM((2, N, N), jnp.int32),
                pltpu.VMEM((2, N, N), F32),
                pltpu.VMEM((HOPS, 2, 2, 2, N, N), BF16),
                pltpu.VMEM((2, 2, 2, N, N), F32),
                pltpu.VMEM((2, 2, 2, H, N), F32),
                pltpu.VMEM((2, 2, 2, N, N), F32),
                pltpu.VMEM((2, NCLASS, 8, 128), F32),
                pltpu.VMEM((2, 2, N, N), BF16),
                pltpu.VMEM((2, 2, N, N), BF16),
                pltpu.VMEM((2, 2 * N, N), BF16),
                pltpu.VMEM((2, N, N), F32),
                pltpu.VMEM((2, N, N), F32),
                pltpu.VMEM((2, groups, rows, N), BF16),
                pltpu.VMEM((2, groups - 1, rows, N), BF16),
                pltpu.SMEM((NCLASS,), F32),
                pltpu.SMEM((2,), jnp.int32),
                dma((7,)),
                dma((HOPS, 2)),
                dma((HOPS, 2, 2)),
                dma((HOPS, 2, 2)),
                dma((2, groups - 1)),
                dma((2, groups - 1)),
                pltpu.SemaphoreType.REGULAR((3,)),
            ],
            compiler_params=pltpu.CompilerParams(
                collective_id=0, has_side_effects=True, vmem_limit_bytes=40 * 1024 * 1024
            ),
        )(
            *(
                pltpu.with_memory_space_constraint(x, pltpu.HBM)
                for x in (
                    screen_values,
                    freq_index,
                    down_state,
                    up_state,
                    source,
                    reflect,
                    screen_class,
                    table,
                )
            ),
        )
        return pl.pallas_call(
            store,
            out_shape=[
                pltpu.HBM(down_state.shape, BF16),
                pltpu.HBM(up_state.shape, BF16),
                pltpu.HBM((2, rows, N), F32),
            ],
            in_specs=[vmem] * 3,
            out_specs=[hbm] * 3,
            scratch_shapes=[dma((5,))],
            compiler_params=pltpu.CompilerParams(vmem_limit_bytes=1024 * 1024),
        )(*(pltpu.with_memory_space_constraint(x, pltpu.VMEM) for x in results))

    return jax.shard_map(
        per_device,
        mesh=mesh,
        in_specs=(
            P("depth", "shot", None, None, None),
            P("depth", "shot", None, None, None),
            P("shot", None, None, None),
            P("depth", None, None),
            P("depth", None, None),
            P(),
            P("shot"),
        ),
        out_specs=(
            P("depth", "shot", None, None, None),
            P("depth", "shot", None, None, None),
            P("depth", "shot", None),
        ),
        check_vma=False,
    )
```

```python
import math

import jax
import jax.numpy as jnp
import numpy as np
from jax import lax
from jax.experimental import pallas as pl
from jax.experimental.pallas import tpu as pltpu
from jax.sharding import PartitionSpec as P

HOPS = 3
NCLASS = 16
NFREQ = 128
N = 256
H = N // 2
MESH = pl.DeviceIdType.MESH
BF16 = jnp.bfloat16
F32 = jnp.float32
COS_COEFS = [(-1.0) ** k / math.factorial(2 * k) for k in range(10)]
SIN_COEFS = [(-1.0) ** k / math.factorial(2 * k + 1) for k in range(10)]


def half_tables():
    row = np.arange(H)[:, None]
    col = np.arange(H)[None, :]
    mats = []
    for parity in (0, 1):
        angle = (2.0 * math.pi / N) * (((2 * row + parity) * col) % N).astype(np.float64)
        cos, sin = np.cos(angle), np.sin(angle)
        fwd = np.block([[cos, sin], [-sin, cos]])
        mats.append(fwd)
        mats.append(fwd.T)
    return np.stack(mats).astype(np.float32)


def poly(coefs, q):
    acc = jnp.full_like(q, coefs[-1])
    for c in coefs[-2::-1]:
        acc = acc * q + c
    return acc


def dot(a, b):
    return jnp.dot(a, b, preferred_element_type=F32)


def kernel(
    groups,
    slabs,
    values_hbm,
    freq_hbm,
    down_hbm,
    up_hbm,
    source_hbm,
    reflect_hbm,
    class_hbm,
    table_hbm,
    local,
    edge,
    grad_out,
    tab,
    classes,
    refl,
    halo,
    inner,
    phase,
    screen,
    lut,
    s2,
    s3,
    s4,
    gsum,
    final_x,
    gsend,
    grecv,
    screen_values,
    freq_index,
    load_sem,
    src_sem,
    send_sem,
    recv_sem,
    gsend_sem,
    grecv_sem,
    near_sem,
):
    d = lax.axis_index("depth")
    s = lax.axis_index("shot")
    has_above = d > 0
    has_below = d < slabs - 1

    loads = [
        pltpu.make_async_copy(table_hbm, tab, load_sem.at[0]),
        pltpu.make_async_copy(class_hbm, classes, load_sem.at[1]),
        pltpu.make_async_copy(reflect_hbm, refl, load_sem.at[2]),
        pltpu.make_async_copy(down_hbm.at[0], local.at[0], load_sem.at[3]),
        pltpu.make_async_copy(up_hbm.at[1], local.at[1], load_sem.at[4]),
        pltpu.make_async_copy(freq_hbm, freq_index, load_sem.at[5]),
        pltpu.make_async_copy(values_hbm, screen_values, load_sem.at[6]),
    ]
    near = [
        lax.rem(s + 2, groups),
        lax.rem(s + groups - 2, groups),
        s + 1 - 2 * lax.rem(s, 2),
    ]

    def greet(sem):
        for peer in near:
            pl.semaphore_signal(sem, inc=1, device_id={"shot": peer}, device_id_type=MESH)

    barrier = pltpu.get_barrier_semaphore()

    @pl.when(has_above)
    def _():
        pl.semaphore_signal(barrier, inc=1, device_id={"depth": d - 1}, device_id_type=MESH)

    @pl.when(has_below)
    def _():
        pl.semaphore_signal(barrier, inc=1, device_id={"depth": d + 1}, device_id_type=MESH)

    greet(barrier)
    for c in loads[::-1]:
        c.start()

    def link(src, h, k, f):
        return pltpu.make_async_remote_copy(
            src_ref=src,
            dst_ref=halo.at[h, 1 - k, f],
            send_sem=send_sem.at[h, k, f],
            recv_sem=recv_sem.at[h, 1 - k, f],
            device_id={"depth": lax.rem(d + 2 * k + slabs - 1, slabs)},
            device_id_type=MESH,
        )

    def linked(k):
        peer = d + 2 * k - 1
        return jnp.logical_and(peer >= 0, peer < slabs)

    def from_source(h, f):
        return pltpu.make_async_copy(source_hbm.at[f], halo.at[h, 0, f], src_sem.at[h, f])

    late = lax.rem(d, 2)
    early = 1 - late

    def fill_phase(t, carry):
        r0 = pl.multiple_of(t * 8, 8)
        row = lax.broadcasted_iota(jnp.int32, (8, N), 0) + r0
        lane = lax.broadcasted_iota(jnp.int32, (8, N), 1)
        ym = jnp.where(lane < H, 2 * lane, 2 * (lane - H) + 1)
        ym = jnp.where(ym >= H, ym - N, ym)
        ky = (2.0 * math.pi / N) * ym.astype(F32)
        for par in range(2):
            xm = 2 * row + par
            xm = jnp.where(xm >= H, xm - N, xm)
            kx = (2.0 * math.pi / N) * xm.astype(F32)
            k2 = kx * kx + ky * ky
            for f in range(2):
                q = kwave[f] * kwave[f] - k2
                root = jnp.sqrt(jnp.abs(q))
                qp = jnp.maximum(q, 0.0)
                damp = jnp.where(q < 0.0, jnp.exp(-root), 1.0) * (1.0 / (N * N))
                sin = jnp.where(q > 0.0, root, 0.0) * poly(SIN_COEFS, qp)
                phase[f, par, 0, pl.ds(r0, 8), :] = damp * poly(COS_COEFS, qp)
                phase[f, par, 1, pl.ds(r0, 8), :] = damp * sin
        return carry

    def fill_screen(f):
        k0 = 0.95 * math.pi * (freq_index[f].astype(F32) + 1.0) / NFREQ
        for c in range(NCLASS):
            ang = jnp.full((8, 128), k0 * screen_values[c], F32)
            q = ang * ang
            lut[0, c] = poly(COS_COEFS, q)
            lut[1, c] = ang * poly(SIN_COEFS, q)

        def rows(t, carry):
            lev = t // (N // 32)
            r0 = pl.multiple_of(lax.rem(t, N // 32) * 32, 32)
            tables = [[lut[k, c] for c in range(NCLASS)] for k in range(2)]
            for i in range(4):
                for j in range(2):
                    here = (pl.ds(r0 + 8 * i, 8), pl.ds(j * H, H))
                    cls = classes[lev, *here]
                    bits = [(cls & (1 << b)) != 0 for b in range(4)]
                    for k in range(2):
                        vals = tables[k]
                        for bit in bits:
                            vals = [
                                jnp.where(bit, vals[2 * m + 1], vals[2 * m])
                                for m in range(len(vals) // 2)
                            ]
                        screen[lev, f, k, *here] = vals[0]
            return carry

        lax.fori_loop(0, 2 * N // 32, rows, 0)

    loads[5].wait()
    kwave = [0.95 * math.pi * (freq_index[f].astype(F32) + 1.0) / NFREQ for f in range(2)]
    lax.fori_loop(0, H // 8, fill_phase, 0)
    pl.semaphore_wait(
        barrier, len(near) + has_above.astype(jnp.int32) + has_below.astype(jnp.int32)
    )

    for f in range(2):

        @pl.when(has_above)
        def _():
            link(up_hbm.at[0, f], 0, 0, f).start()

        @pl.when(has_below)
        def _():
            link(down_hbm.at[1, f], 0, 1, f).start()

    @pl.when(jnp.logical_not(has_above))
    def _():
        for h in range(HOPS):
            for f in range(2):
                from_source(h, f).start()

    @pl.when(jnp.logical_not(has_below))
    def _():
        def clear(t, carry):
            halo[t // 2, 1, lax.rem(t, 2)] = jnp.zeros((2, N, N), BF16)
            return carry

        lax.fori_loop(0, 2 * HOPS, clear, 0)

    greet(near_sem.at[0])

    def propagate(srcs, f):
        fe, ie, fo, io = 0, 1, 2, 3
        n = len(srcs)
        sums, difs = [], []
        for src in srcs:
            re_l, re_r = src[0, :, :H], src[0, :, H:]
            im_l, im_r = src[1, :, :H], src[1, :, H:]
            sums.append(jnp.concatenate([re_l + re_r, im_l + im_r], axis=1))
            difs.append(jnp.concatenate([re_l - re_r, im_l - im_r], axis=1))
        ev = dot(jnp.concatenate(sums, axis=0), tab[ie])
        od = dot(jnp.concatenate(difs, axis=0), tab[io])
        for i in range(n):
            for j, x in enumerate((ev[i * N : (i + 1) * N], od[i * N : (i + 1) * N])):
                cols = slice(j * H, (j + 1) * H)
                u = (x[:H] + x[H:]).astype(BF16)
                v = (x[:H] - x[H:]).astype(BF16)
                s2[i, 0, :H, cols] = u[:, :H]
                s2[i, 0, H:, cols] = u[:, H:]
                s2[i, 1, :H, cols] = v[:, :H]
                s2[i, 1, H:, cols] = v[:, H:]
        for i in range(n):
            for par, t in enumerate((fe, fo)):
                x = dot(tab[t], s2[i, par])
                pr, pi = phase[f, par, 0], phase[f, par, 1]
                re, im = x[:H], x[H:]
                s3[i, par, :H] = (re * pr - im * pi).astype(BF16)
                s3[i, par, H:] = (re * pi + im * pr).astype(BF16)
        for i in range(n):
            e = dot(tab[ie], s3[i, 0])
            o = dot(tab[io], s3[i, 1])
            top = (e + o).astype(BF16)
            bot = (e - o).astype(BF16)
            lo, hi = slice(i * N, i * N + H), slice(i * N + H, i * N + N)
            for j in range(2):
                cols = slice(j * H, (j + 1) * H)
                s4[j, lo, :H] = top[:H, cols]
                s4[j, lo, H:] = top[H:, cols]
                s4[j, hi, :H] = bot[:H, cols]
                s4[j, hi, H:] = bot[H:, cols]
        e = dot(s4[0, : n * N], tab[fe])
        o = dot(s4[1, : n * N], tab[fo])
        sm, df = e + o, e - o
        return [(sm[i * N : (i + 1) * N], df[i * N : (i + 1) * N]) for i in range(n)]

    def screened(x, lev, f, j):
        cols = slice(j * H, (j + 1) * H)
        sr, si = screen[lev, f, 0, :, cols], screen[lev, f, 1, :, cols]
        re, im = x[j][:, :H], x[j][:, H:]
        return (sr * re - si * im, sr * im + si * re)

    def inner_step(f):
        for i, q in enumerate(propagate((local.at[0, f], local.at[1, f]), f)):
            for j in range(2):
                cols = slice(j * H, (j + 1) * H)
                for c, x in enumerate(screened(q, 1 - i, f, j)):
                    inner[1 - i, f, c, :, cols] = x

    rows = N // groups
    scale = 1.0 / math.sqrt(2 * groups)

    def wait_halo(h, k, f):
        @pl.when(linked(k))
        def _():
            link(halo.at[h, k, f], h, 1 - k, f).wait_recv()

        @pl.when(jnp.logical_and(d == 0, k == 0))
        def _():
            from_source(h, f).wait()

    def meet(q, h, k, f, keep):
        for j in range(2):
            cols = slice(j * H, (j + 1) * H)
            r = refl[k, :, cols]
            xs = screened(q, k, f, j)
            g = None
            for c in range(2):
                x, y = xs[c], inner[k, f, c, :, cols]
                t = r * (x - y)
                edge[h, k, f, c, :, cols] = (y + t).astype(BF16)
                local[k, f, c, :, cols] = (x + t).astype(BF16)
                g = x * y if g is None else g + x * y
            if keep:
                gsum[k, :, cols] = g

    def meet_last(q, h, k, f):
        for j in range(2):
            cols = slice(j * H, (j + 1) * H)
            re, im = screened(q, k, f, j)
            final_x[0, :, cols] = re
            final_x[1, :, cols] = im
            g = re * inner[k, f, 0, :, cols] + im * inner[k, f, 1, :, cols]
            out = ((gsum[k, :, cols] + g) * scale).astype(BF16)
            for p in range(groups):
                gsend[k, p, :, cols] = out[p * rows : (p + 1) * rows]
        for i in same_y:
            share(k, i).start()

        @pl.when(jnp.logical_not(holds))
        def _():
            for i in cross_y:
                share(k, i).start()

        for c in range(2):
            x, y = final_x[c], inner[k, f, c]
            t = refl[k] * (x - y)
            edge[h, k, f, c] = (y + t).astype(BF16)
            local[k, f, c] = (x + t).astype(BF16)

    def send(h, k, f):
        @pl.when(linked(k))
        def _():
            link(edge.at[h, k, f], h + 1, k, f).start()

    mate = s + 1 - 2 * lax.rem(s, 2)

    def over(p, o):
        return lax.rem(p + o, groups)

    peers = [over(mate, 4), over(mate, 2), over(mate, 6), over(s, 4), mate, over(s, 2), over(s, 6)]

    cross_y = (0, 1, 2, 4)
    same_y = (3, 5, 6)
    holds = d < 2

    def share(k, i):
        return pltpu.make_async_remote_copy(
            src_ref=gsend.at[k, peers[i]],
            dst_ref=grecv.at[k, i],
            send_sem=gsend_sem.at[k, i],
            recv_sem=grecv_sem.at[k, i],
            device_id={"shot": peers[i]},
            device_id_type=MESH,
        )

    loads[6].wait()
    loads[1].wait()
    loads[2].wait()
    fill_screen(0)
    refl[1] = -refl[1]
    loads[0].wait()
    loads[3].wait()
    loads[4].wait()

    def first(f, carry):
        @pl.when(f == 1)
        def _():
            fill_screen(1)

        inner_step(f)
        return carry

    lax.fori_loop(0, 2, first, 0)
    pl.semaphore_wait(near_sem.at[0], len(near))
    greet(near_sem.at[1])

    def pair(h, f):
        wait_halo(h, early, f)
        wait_halo(h, late, f)
        return propagate((halo.at[h, late, f], halo.at[h, early, f]), f)

    def middle(t, carry):
        h, f = t // 2, lax.rem(t, 2)
        ql, qe = pair(h, f)
        meet(ql, h, late, f, False)
        send(h, late, f)
        meet(qe, h, early, f, False)
        send(h, early, f)
        inner_step(f)
        return carry

    lax.fori_loop(0, 2 * (HOPS - 1), middle, 0)
    pl.semaphore_wait(near_sem.at[1], len(near))

    end = HOPS - 1
    ql, qe = pair(end, 0)
    meet(ql, end, late, 0, True)
    meet(qe, end, early, 0, True)

    def final(t, carry):
        k = early + t * (late - early)
        wait_halo(end, k, 1)
        (q,) = propagate((halo.at[end, k, 1],), 1)
        meet_last(q, end, k, 1)
        return carry

    lax.fori_loop(0, 2, final, 0)

    @pl.when(holds)
    def _():
        for k in range(2):
            for i in same_y:
                share(k, i).wait_recv()
        for k in range(2):
            for i in cross_y:
                share(k, i).start()

    @pl.when(jnp.logical_not(holds))
    def _():
        for k in range(2):
            for i in same_y:
                share(k, i).wait_recv()

    for h in range(HOPS):
        for k in range(2):
            for f in range(2):

                @pl.when(linked(k))
                def _():
                    link(edge.at[0, k, f], h, k, f).wait_send()

    for k in (early, late):
        for i in cross_y:
            share(k, i).wait_recv()
        total = gsend[k, s].astype(F32)
        for i in range(groups - 1):
            total = total + grecv[k, i].astype(F32)
        grad_out[k] = total
    for k in range(2):
        for i in range(groups - 1):
            share(k, i).wait_send()


def store(local, edge, grad, down_out, up_out, grad_out, sems):
    last = edge.shape[0] - 1
    pairs = [
        (local.at[0], down_out.at[0]),
        (edge.at[last, 1], down_out.at[1]),
        (edge.at[last, 0], up_out.at[0]),
        (local.at[1], up_out.at[1]),
        (grad, grad_out),
    ]
    copies = [pltpu.make_async_copy(a, b, sems.at[i]) for i, (a, b) in enumerate(pairs)]
    for c in copies:
        c.start()
    for c in copies:
        c.wait()


def solution(mesh):
    groups = mesh.shape["shot"]
    slabs = mesh.shape["depth"]
    rows = N // groups

    def per_device(down_state, up_state, source, reflect, screen_class, screen_values, freq_index):
        table = jnp.asarray(half_tables(), BF16)
        hbm = pl.BlockSpec(memory_space=pltpu.HBM)
        vmem = pl.BlockSpec(memory_space=pltpu.VMEM)
        dma = pltpu.SemaphoreType.DMA
        results = pl.pallas_call(
            lambda *refs: kernel(groups, slabs, *refs),
            out_shape=(
                pltpu.VMEM((2, 2, 2, N, N), BF16),
                pltpu.VMEM((HOPS, 2, 2, 2, N, N), BF16),
                pltpu.VMEM((2, rows, N), F32),
            ),
            in_specs=[hbm] * 8,
            out_specs=(vmem, vmem, vmem),
            scratch_shapes=[
                pltpu.VMEM((4, N, N), BF16),
                pltpu.VMEM((2, N, N), jnp.int32),
                pltpu.VMEM((2, N, N), F32),
                pltpu.VMEM((HOPS, 2, 2, 2, N, N), BF16),
                pltpu.VMEM((2, 2, 2, N, N), F32),
                pltpu.VMEM((2, 2, 2, H, N), F32),
                pltpu.VMEM((2, 2, 2, N, N), F32),
                pltpu.VMEM((2, NCLASS, 8, 128), F32),
                pltpu.VMEM((2, 2, N, N), BF16),
                pltpu.VMEM((2, 2, N, N), BF16),
                pltpu.VMEM((2, 2 * N, N), BF16),
                pltpu.VMEM((2, N, N), F32),
                pltpu.VMEM((2, N, N), F32),
                pltpu.VMEM((2, groups, rows, N), BF16),
                pltpu.VMEM((2, groups - 1, rows, N), BF16),
                pltpu.SMEM((NCLASS,), F32),
                pltpu.SMEM((2,), jnp.int32),
                dma((7,)),
                dma((HOPS, 2)),
                dma((HOPS, 2, 2)),
                dma((HOPS, 2, 2)),
                dma((2, groups - 1)),
                dma((2, groups - 1)),
                pltpu.SemaphoreType.REGULAR((2,)),
            ],
            compiler_params=pltpu.CompilerParams(
                collective_id=0, has_side_effects=True, vmem_limit_bytes=40 * 1024 * 1024
            ),
        )(
            *(
                pltpu.with_memory_space_constraint(x, pltpu.HBM)
                for x in (
                    screen_values,
                    freq_index,
                    down_state,
                    up_state,
                    source,
                    reflect,
                    screen_class,
                    table,
                )
            ),
        )
        return pl.pallas_call(
            store,
            out_shape=[
                pltpu.HBM(down_state.shape, BF16),
                pltpu.HBM(up_state.shape, BF16),
                pltpu.HBM((2, rows, N), F32),
            ],
            in_specs=[vmem] * 3,
            out_specs=[hbm] * 3,
            scratch_shapes=[dma((5,))],
            compiler_params=pltpu.CompilerParams(vmem_limit_bytes=1024 * 1024),
        )(*(pltpu.with_memory_space_constraint(x, pltpu.VMEM) for x in results))

    return jax.shard_map(
        per_device,
        mesh=mesh,
        in_specs=(
            P("depth", "shot", None, None, None),
            P("depth", "shot", None, None, None),
            P("shot", None, None, None),
            P("depth", None, None),
            P("depth", None, None),
            P(),
            P("shot"),
        ),
        out_specs=(
            P("depth", "shot", None, None, None),
            P("depth", "shot", None, None, None),
            P("depth", "shot", None),
        ),
        check_vma=False,
    )
```

```python
import math

import jax
import jax.numpy as jnp
import numpy as np
from jax import lax
from jax.experimental import pallas as pl
from jax.experimental.pallas import tpu as pltpu
from jax.sharding import PartitionSpec as P

HOPS = 3
NCLASS = 16
NFREQ = 128
N = 256
H = N // 2
MESH = pl.DeviceIdType.MESH
BF16 = jnp.bfloat16
F32 = jnp.float32
COS_COEFS = [(-1.0) ** k / math.factorial(2 * k) for k in range(10)]
SIN_COEFS = [(-1.0) ** k / math.factorial(2 * k + 1) for k in range(10)]


def half_tables():
    row = np.arange(H)[:, None]
    col = np.arange(H)[None, :]
    mats = []
    for parity in (0, 1):
        angle = (2.0 * math.pi / N) * (((2 * row + parity) * col) % N).astype(np.float64)
        cos, sin = np.cos(angle), np.sin(angle)
        fwd = np.block([[cos, sin], [-sin, cos]])
        mats.append(fwd)
        mats.append(fwd.T)
    return np.stack(mats).astype(np.float32)


def poly(coefs, q):
    acc = jnp.full_like(q, coefs[-1])
    for c in coefs[-2::-1]:
        acc = acc * q + c
    return acc


def dot(a, b):
    return jnp.dot(a, b, preferred_element_type=F32)


def kernel(
    groups,
    slabs,
    values_hbm,
    freq_hbm,
    down_hbm,
    up_hbm,
    source_hbm,
    reflect_hbm,
    class_hbm,
    table_hbm,
    local,
    edge,
    grad_out,
    tab,
    classes,
    refl,
    halo,
    inner,
    phase,
    screen,
    lut,
    s2,
    s3,
    s4,
    gsum,
    final_x,
    gsend,
    grecv,
    screen_values,
    freq_index,
    load_sem,
    src_sem,
    send_sem,
    recv_sem,
    gsend_sem,
    grecv_sem,
    near_sem,
):
    d = lax.axis_index("depth")
    s = lax.axis_index("shot")
    has_above = d > 0
    has_below = d < slabs - 1

    loads = [
        pltpu.make_async_copy(table_hbm, tab, load_sem.at[0]),
        pltpu.make_async_copy(class_hbm, classes, load_sem.at[1]),
        pltpu.make_async_copy(reflect_hbm, refl, load_sem.at[2]),
        pltpu.make_async_copy(down_hbm.at[0], local.at[0], load_sem.at[3]),
        pltpu.make_async_copy(up_hbm.at[1], local.at[1], load_sem.at[4]),
        pltpu.make_async_copy(freq_hbm, freq_index, load_sem.at[5]),
        pltpu.make_async_copy(values_hbm, screen_values, load_sem.at[6]),
    ]
    near = [
        lax.rem(s + 2, groups),
        lax.rem(s + groups - 2, groups),
        s + 1 - 2 * lax.rem(s, 2),
    ]

    def greet(sem):
        for peer in near:
            pl.semaphore_signal(sem, inc=1, device_id={"shot": peer}, device_id_type=MESH)

    barrier = pltpu.get_barrier_semaphore()

    @pl.when(has_above)
    def _():
        pl.semaphore_signal(barrier, inc=1, device_id={"depth": d - 1}, device_id_type=MESH)

    @pl.when(has_below)
    def _():
        pl.semaphore_signal(barrier, inc=1, device_id={"depth": d + 1}, device_id_type=MESH)

    greet(barrier)
    for c in loads[::-1]:
        c.start()

    def link(src, h, k, f):
        return pltpu.make_async_remote_copy(
            src_ref=src,
            dst_ref=halo.at[h, 1 - k, f],
            send_sem=send_sem.at[h, k, f],
            recv_sem=recv_sem.at[h, 1 - k, f],
            device_id={"depth": lax.rem(d + 2 * k + slabs - 1, slabs)},
            device_id_type=MESH,
        )

    def linked(k):
        peer = d + 2 * k - 1
        return jnp.logical_and(peer >= 0, peer < slabs)

    def from_source(h, f):
        return pltpu.make_async_copy(source_hbm.at[f], halo.at[h, 0, f], src_sem.at[h, f])

    late = lax.rem(d, 2)
    early = 1 - late

    def fill_phase(t, carry):
        r0 = pl.multiple_of(t * 8, 8)
        row = lax.broadcasted_iota(jnp.int32, (8, N), 0) + r0
        lane = lax.broadcasted_iota(jnp.int32, (8, N), 1)
        ym = jnp.where(lane < H, 2 * lane, 2 * (lane - H) + 1)
        ym = jnp.where(ym >= H, ym - N, ym)
        ky = (2.0 * math.pi / N) * ym.astype(F32)
        for par in range(2):
            xm = 2 * row + par
            xm = jnp.where(xm >= H, xm - N, xm)
            kx = (2.0 * math.pi / N) * xm.astype(F32)
            k2 = kx * kx + ky * ky
            for f in range(2):
                q = kwave[f] * kwave[f] - k2
                root = jnp.sqrt(jnp.abs(q))
                qp = jnp.maximum(q, 0.0)
                damp = jnp.where(q < 0.0, jnp.exp(-root), 1.0) * (1.0 / (N * N))
                sin = jnp.where(q > 0.0, root, 0.0) * poly(SIN_COEFS, qp)
                phase[f, par, 0, pl.ds(r0, 8), :] = damp * poly(COS_COEFS, qp)
                phase[f, par, 1, pl.ds(r0, 8), :] = damp * sin
        return carry

    def fill_screen(f):
        k0 = 0.95 * math.pi * (freq_index[f].astype(F32) + 1.0) / NFREQ
        for c in range(NCLASS):
            ang = jnp.full((8, 128), k0 * screen_values[c], F32)
            q = ang * ang
            lut[0, c] = poly(COS_COEFS, q)
            lut[1, c] = ang * poly(SIN_COEFS, q)

        def rows(t, carry):
            lev = t // (N // 32)
            r0 = pl.multiple_of(lax.rem(t, N // 32) * 32, 32)
            tables = [[lut[k, c] for c in range(NCLASS)] for k in range(2)]
            for i in range(4):
                for j in range(2):
                    here = (pl.ds(r0 + 8 * i, 8), pl.ds(j * H, H))
                    cls = classes[lev, *here]
                    bits = [(cls & (1 << b)) != 0 for b in range(4)]
                    for k in range(2):
                        vals = tables[k]
                        for bit in bits:
                            vals = [
                                jnp.where(bit, vals[2 * m + 1], vals[2 * m])
                                for m in range(len(vals) // 2)
                            ]
                        screen[lev, f, k, *here] = vals[0]
            return carry

        lax.fori_loop(0, 2 * N // 32, rows, 0)

    loads[5].wait()
    kwave = [0.95 * math.pi * (freq_index[f].astype(F32) + 1.0) / NFREQ for f in range(2)]
    lax.fori_loop(0, H // 8, fill_phase, 0)
    pl.semaphore_wait(
        barrier, len(near) + has_above.astype(jnp.int32) + has_below.astype(jnp.int32)
    )

    for f in range(2):

        @pl.when(has_above)
        def _():
            link(up_hbm.at[0, f], 0, 0, f).start()

        @pl.when(has_below)
        def _():
            link(down_hbm.at[1, f], 0, 1, f).start()

    @pl.when(jnp.logical_not(has_above))
    def _():
        for h in range(HOPS):
            for f in range(2):
                from_source(h, f).start()

    @pl.when(jnp.logical_not(has_below))
    def _():
        def clear(t, carry):
            halo[t // 2, 1, lax.rem(t, 2)] = jnp.zeros((2, N, N), BF16)
            return carry

        lax.fori_loop(0, 2 * HOPS, clear, 0)

    greet(near_sem.at[0])

    def propagate(srcs, f):
        fe, ie, fo, io = 0, 1, 2, 3
        n = len(srcs)
        sums, difs = [], []
        for src in srcs:
            re_l, re_r = src[0, :, :H], src[0, :, H:]
            im_l, im_r = src[1, :, :H], src[1, :, H:]
            sums.append(jnp.concatenate([re_l + re_r, im_l + im_r], axis=1))
            difs.append(jnp.concatenate([re_l - re_r, im_l - im_r], axis=1))
        ev = dot(jnp.concatenate(sums, axis=0), tab[ie])
        od = dot(jnp.concatenate(difs, axis=0), tab[io])
        for i in range(n):
            for j, x in enumerate((ev[i * N : (i + 1) * N], od[i * N : (i + 1) * N])):
                cols = slice(j * H, (j + 1) * H)
                u = (x[:H] + x[H:]).astype(BF16)
                v = (x[:H] - x[H:]).astype(BF16)
                s2[i, 0, :H, cols] = u[:, :H]
                s2[i, 0, H:, cols] = u[:, H:]
                s2[i, 1, :H, cols] = v[:, :H]
                s2[i, 1, H:, cols] = v[:, H:]
        for i in range(n):
            for par, t in enumerate((fe, fo)):
                x = dot(tab[t], s2[i, par])
                pr, pi = phase[f, par, 0], phase[f, par, 1]
                re, im = x[:H], x[H:]
                s3[i, par, :H] = (re * pr - im * pi).astype(BF16)
                s3[i, par, H:] = (re * pi + im * pr).astype(BF16)
        for i in range(n):
            e = dot(tab[ie], s3[i, 0])
            o = dot(tab[io], s3[i, 1])
            top = (e + o).astype(BF16)
            bot = (e - o).astype(BF16)
            lo, hi = slice(i * N, i * N + H), slice(i * N + H, i * N + N)
            for j in range(2):
                cols = slice(j * H, (j + 1) * H)
                s4[j, lo, :H] = top[:H, cols]
                s4[j, lo, H:] = top[H:, cols]
                s4[j, hi, :H] = bot[:H, cols]
                s4[j, hi, H:] = bot[H:, cols]
        e = dot(s4[0, : n * N], tab[fe])
        o = dot(s4[1, : n * N], tab[fo])
        sm, df = e + o, e - o
        return [(sm[i * N : (i + 1) * N], df[i * N : (i + 1) * N]) for i in range(n)]

    def screened(x, lev, f, j):
        cols = slice(j * H, (j + 1) * H)
        sr, si = screen[lev, f, 0, :, cols], screen[lev, f, 1, :, cols]
        re, im = x[j][:, :H], x[j][:, H:]
        return (sr * re - si * im, sr * im + si * re)

    def inner_step(f):
        for i, q in enumerate(propagate((local.at[0, f], local.at[1, f]), f)):
            for j in range(2):
                cols = slice(j * H, (j + 1) * H)
                for c, x in enumerate(screened(q, 1 - i, f, j)):
                    inner[1 - i, f, c, :, cols] = x

    rows = N // groups
    scale = 1.0 / math.sqrt(2 * groups)

    def wait_halo(h, k, f):
        @pl.when(linked(k))
        def _():
            link(halo.at[h, k, f], h, 1 - k, f).wait_recv()

        @pl.when(jnp.logical_and(d == 0, k == 0))
        def _():
            from_source(h, f).wait()

    def meet(q, h, k, f, keep):
        for j in range(2):
            cols = slice(j * H, (j + 1) * H)
            r = refl[k, :, cols]
            xs = screened(q, k, f, j)
            g = None
            for c in range(2):
                x, y = xs[c], inner[k, f, c, :, cols]
                t = r * (x - y)
                edge[h, k, f, c, :, cols] = (y + t).astype(BF16)
                local[k, f, c, :, cols] = (x + t).astype(BF16)
                g = x * y if g is None else g + x * y
            if keep:
                gsum[k, :, cols] = g

    def meet_last(q, h, k, f):
        for j in range(2):
            cols = slice(j * H, (j + 1) * H)
            re, im = screened(q, k, f, j)
            final_x[0, :, cols] = re
            final_x[1, :, cols] = im
            g = re * inner[k, f, 0, :, cols] + im * inner[k, f, 1, :, cols]
            out = ((gsum[k, :, cols] + g) * scale).astype(BF16)
            for p in range(groups):
                gsend[k, p, :, cols] = out[p * rows : (p + 1) * rows]

        @pl.when(jnp.logical_not(holds))
        def _():
            for i in cross_y:
                share(k, i).start()

        for i in same_y:
            share(k, i).start()
        for c in range(2):
            x, y = final_x[c], inner[k, f, c]
            t = refl[k] * (x - y)
            edge[h, k, f, c] = (y + t).astype(BF16)
            local[k, f, c] = (x + t).astype(BF16)

    def send(h, k, f):
        @pl.when(linked(k))
        def _():
            link(edge.at[h, k, f], h + 1, k, f).start()

    mate = s + 1 - 2 * lax.rem(s, 2)

    def over(p, o):
        return lax.rem(p + o, groups)

    peers = [over(mate, 4), over(mate, 2), over(mate, 6), over(s, 4), mate, over(s, 2), over(s, 6)]

    cross_y = (0, 1, 2, 4)
    same_y = (3, 5, 6)
    holds = d < 2

    def share(k, i):
        return pltpu.make_async_remote_copy(
            src_ref=gsend.at[k, peers[i]],
            dst_ref=grecv.at[k, i],
            send_sem=gsend_sem.at[k, i],
            recv_sem=grecv_sem.at[k, i],
            device_id={"shot": peers[i]},
            device_id_type=MESH,
        )

    loads[6].wait()
    loads[1].wait()
    loads[2].wait()
    fill_screen(0)
    refl[1] = -refl[1]
    loads[0].wait()
    loads[3].wait()
    loads[4].wait()

    def first(f, carry):
        @pl.when(f == 1)
        def _():
            fill_screen(1)

        inner_step(f)
        return carry

    lax.fori_loop(0, 2, first, 0)
    pl.semaphore_wait(near_sem.at[0], len(near))
    greet(near_sem.at[1])

    def pair(h, f):
        wait_halo(h, early, f)
        wait_halo(h, late, f)
        return propagate((halo.at[h, late, f], halo.at[h, early, f]), f)

    def middle(t, carry):
        h, f = t // 2, lax.rem(t, 2)
        ql, qe = pair(h, f)
        meet(ql, h, late, f, False)
        send(h, late, f)
        meet(qe, h, early, f, False)
        send(h, early, f)
        inner_step(f)
        return carry

    lax.fori_loop(0, 2 * (HOPS - 1), middle, 0)
    pl.semaphore_wait(near_sem.at[1], len(near))

    end = HOPS - 1
    ql, qe = pair(end, 0)
    meet(ql, end, late, 0, True)
    meet(qe, end, early, 0, True)

    def final(t, carry):
        k = early + t * (late - early)
        wait_halo(end, k, 1)
        (q,) = propagate((halo.at[end, k, 1],), 1)
        meet_last(q, end, k, 1)
        return carry

    lax.fori_loop(0, 2, final, 0)

    @pl.when(holds)
    def _():
        for k in range(2):
            for i in same_y:
                share(k, i).wait_recv()
        for k in range(2):
            for i in cross_y:
                share(k, i).start()

    @pl.when(jnp.logical_not(holds))
    def _():
        for k in range(2):
            for i in same_y:
                share(k, i).wait_recv()

    for h in range(HOPS):
        for k in range(2):
            for f in range(2):

                @pl.when(linked(k))
                def _():
                    link(edge.at[0, k, f], h, k, f).wait_send()

    for k in (early, late):
        for i in cross_y:
            share(k, i).wait_recv()
        total = gsend[k, s].astype(F32)
        for i in range(groups - 1):
            total = total + grecv[k, i].astype(F32)
        grad_out[k] = total
    for k in range(2):
        for i in range(groups - 1):
            share(k, i).wait_send()


def store(local, edge, grad, down_out, up_out, grad_out, sems):
    last = edge.shape[0] - 1
    pairs = [
        (local.at[0], down_out.at[0]),
        (edge.at[last, 1], down_out.at[1]),
        (edge.at[last, 0], up_out.at[0]),
        (local.at[1], up_out.at[1]),
        (grad, grad_out),
    ]
    copies = [pltpu.make_async_copy(a, b, sems.at[i]) for i, (a, b) in enumerate(pairs)]
    for c in copies:
        c.start()
    for c in copies:
        c.wait()


def solution(mesh):
    groups = mesh.shape["shot"]
    slabs = mesh.shape["depth"]
    rows = N // groups

    def per_device(down_state, up_state, source, reflect, screen_class, screen_values, freq_index):
        table = jnp.asarray(half_tables(), BF16)
        hbm = pl.BlockSpec(memory_space=pltpu.HBM)
        vmem = pl.BlockSpec(memory_space=pltpu.VMEM)
        dma = pltpu.SemaphoreType.DMA
        results = pl.pallas_call(
            lambda *refs: kernel(groups, slabs, *refs),
            out_shape=(
                pltpu.VMEM((2, 2, 2, N, N), BF16),
                pltpu.VMEM((HOPS, 2, 2, 2, N, N), BF16),
                pltpu.VMEM((2, rows, N), F32),
            ),
            in_specs=[hbm] * 8,
            out_specs=(vmem, vmem, vmem),
            scratch_shapes=[
                pltpu.VMEM((4, N, N), BF16),
                pltpu.VMEM((2, N, N), jnp.int32),
                pltpu.VMEM((2, N, N), F32),
                pltpu.VMEM((HOPS, 2, 2, 2, N, N), BF16),
                pltpu.VMEM((2, 2, 2, N, N), F32),
                pltpu.VMEM((2, 2, 2, H, N), F32),
                pltpu.VMEM((2, 2, 2, N, N), F32),
                pltpu.VMEM((2, NCLASS, 8, 128), F32),
                pltpu.VMEM((2, 2, N, N), BF16),
                pltpu.VMEM((2, 2, N, N), BF16),
                pltpu.VMEM((2, 2 * N, N), BF16),
                pltpu.VMEM((2, N, N), F32),
                pltpu.VMEM((2, N, N), F32),
                pltpu.VMEM((2, groups, rows, N), BF16),
                pltpu.VMEM((2, groups - 1, rows, N), BF16),
                pltpu.SMEM((NCLASS,), F32),
                pltpu.SMEM((2,), jnp.int32),
                dma((7,)),
                dma((HOPS, 2)),
                dma((HOPS, 2, 2)),
                dma((HOPS, 2, 2)),
                dma((2, groups - 1)),
                dma((2, groups - 1)),
                pltpu.SemaphoreType.REGULAR((2,)),
            ],
            compiler_params=pltpu.CompilerParams(
                collective_id=0, has_side_effects=True, vmem_limit_bytes=40 * 1024 * 1024
            ),
        )(
            *(
                pltpu.with_memory_space_constraint(x, pltpu.HBM)
                for x in (
                    screen_values,
                    freq_index,
                    down_state,
                    up_state,
                    source,
                    reflect,
                    screen_class,
                    table,
                )
            ),
        )
        return pl.pallas_call(
            store,
            out_shape=[
                pltpu.HBM(down_state.shape, BF16),
                pltpu.HBM(up_state.shape, BF16),
                pltpu.HBM((2, rows, N), F32),
            ],
            in_specs=[vmem] * 3,
            out_specs=[hbm] * 3,
            scratch_shapes=[dma((5,))],
            compiler_params=pltpu.CompilerParams(vmem_limit_bytes=1024 * 1024),
        )(*(pltpu.with_memory_space_constraint(x, pltpu.VMEM) for x in results))

    return jax.shard_map(
        per_device,
        mesh=mesh,
        in_specs=(
            P("depth", "shot", None, None, None),
            P("depth", "shot", None, None, None),
            P("shot", None, None, None),
            P("depth", None, None),
            P("depth", None, None),
            P(),
            P("shot"),
        ),
        out_specs=(
            P("depth", "shot", None, None, None),
            P("depth", "shot", None, None, None),
            P("depth", "shot", None),
        ),
        check_vma=False,
    )
```
